128 devices in a mesh: lat: 4 (over y_hi, core), lon: 32 (over x, z, y_lo).
Axes of the slice: x: 4, y: 4 (y_hi: 2, y_lo: 2; y = y_hi * 2 + y_lo), z: 4, core: 2. Of those that a mesh axis runs over, the one named last changes fastest.
Arguments:
- crm_state: bfloat16 [8, 1024, 58, 384], P('lat', 'lon'), may hold values from -4 to 4
- gcm_state: bfloat16 [8, 1024, 6, 72], P('lat', 'lon'), may hold values from -4 to 4
- micro_flags: int32 [8, 1024], P('lat', 'lon'), may hold values 0 or 1
- load_plan: int32 [8, 1024], P('lat', 'lon'), may hold values from 0 to 1023, as said below
- h_mix: bfloat16 [64, 64], replicated, may hold values from -0.75 to 0.75
- v_mix: bfloat16 [58, 58], replicated, may hold values from -0.75 to 0.75
- to_crm: float32 [58, 72], replicated, may hold values from -0.75 to 0.75
- to_gcm: float32 [72, 58], replicated, may hold values from -0.75 to 0.75
- polar_tracer: float32 [8, 72, 1024], P('lat', None, 'lon'), may hold values from -6 to 6
- courant_shift: int32 [8, 72], P('lat'), may hold values from 0 to 1023, as said below
- courant_frac: float32 [8, 72], P('lat'), may hold values from 0 to 1
Outputs:
- new_state: bfloat16 [8, 1024, 58, 384], P('lat', 'lon')
- tendency: float32 [8, 1024, 6, 72], P('lat', 'lon')
- polar_next: float32 [8, 72, 1024], P('lat', None, 'lon')
The draws below stay inside these ranges and needn't reach their ends.
Inputs may be any that keep to these rules, and one draw needn't show every extreme that they name: Each row of load_plan is a permutation of the longitudes; of the 32 longitudes of one aligned block, exactly 1 map into each aligned block of 32 longitudes. `courant_shift`: displacements may be any number of whole cells around the loop; in every row at least one level is displaced by 512 to 543 cells.
All inputs are finite; a program needn't handle non-finite values. No bound on the sum of `micro_flags` on one device may be relied on, other than what follows from the above.
Results may differ from the reference program's by a relative error of at most 0.015.
Values may be sent and summed in bfloat16 or wider, within the bound.
A program may use at most 128 MiB of HBM per device.

```python
import jax
import jax.numpy as jnp
from jax import lax

FIELDS = 6
CRMCOL = 64
CLEV = 58
GLEV = 72
NSUB = 18
CAP = 1
CLON = 32
NLON = 1024
ROWS = 8


def draw_load_plan(key, part):
    blocks = NLON // CLON
    src_keys = jax.random.split(jax.random.fold_in(key, 11), ROWS * blocks)
    dst_keys = jax.random.split(jax.random.fold_in(key, 23), ROWS * blocks)
    src_perm = jax.vmap(lambda k: jax.random.permutation(k, CLON))(src_keys).reshape(ROWS, blocks, CLON).astype(jnp.int32)
    dst_perm = jax.vmap(lambda k: jax.random.permutation(k, CLON))(dst_keys).reshape(ROWS, blocks, CLON).astype(jnp.int32)
    target = src_perm // CAP
    within = src_perm % CAP
    source_block = jnp.arange(blocks, dtype=jnp.int32)[None, :, None]
    pre_slot = source_block * CAP + within
    slot = jnp.take_along_axis(dst_perm.reshape(ROWS, blocks * CLON), (target * CLON + pre_slot).reshape(ROWS, blocks * CLON), axis=1)
    return (target.reshape(ROWS, blocks * CLON) * CLON + slot).astype(jnp.int32)


def draw_courant_shift(key, part):
    general = jax.random.randint(jax.random.fold_in(key, 31), (ROWS, GLEV), 0, NLON, dtype=jnp.int32)
    distant = NLON // 2 + jax.random.randint(jax.random.fold_in(key, 37), (ROWS,), 0, CLON, dtype=jnp.int32)
    chosen_level = jax.random.randint(jax.random.fold_in(key, 41), (ROWS,), 0, GLEV, dtype=jnp.int32)
    levels = jnp.arange(GLEV, dtype=jnp.int32)
    top_level = (chosen_level + 1) % GLEV
    zero_level = (chosen_level + 2) % GLEV
    shaped = jnp.where(levels[None, :] == top_level[:, None], NLON - 1, general)
    shaped = jnp.where(levels[None, :] == zero_level[:, None], 0, shaped)
    return jnp.where(levels[None, :] == chosen_level[:, None], distant[:, None], shaped).astype(jnp.int32)


def set_ends(result, own_key, smallest, top_value):
    index_at = [jax.random.randint(jax.random.fold_in(own_key, axis), (), 0, length) for axis, length in enumerate(result.shape)]
    widest = result.shape.index(max(result.shape))
    beside = index_at[:widest] + [(index_at[widest] + 1) % result.shape[widest]] + index_at[widest + 1:]
    return result.at[tuple(index_at)].set(smallest).at[tuple(beside)].set(top_value)


def level_of(own_key, dims, cuts, least, top_value):
    def one(position, shards_of):
        heights = jax.random.uniform(jax.random.fold_in(jax.random.fold_in(own_key, 6), position), (shards_of,), jnp.float32, least / len(cuts), top_value / len(cuts))
        return jnp.repeat(jnp.exp(heights), dims[position] // shards_of).reshape((-1,) + (1,) * (len(dims) - position - 1))

    gain = one(*cuts[0])
    for cut in cuts[1:]:
        gain = gain * one(*cut)
    return gain


def noise(stream_key, dims, spread, bound, shards=(), held_as=jnp.bfloat16):
    entries = spread * jax.random.normal(stream_key, dims, jnp.float32)
    if shards:
        entries = entries * level_of(stream_key, dims, shards, -0.22, 0.18)
    return jnp.clip(entries, -bound, bound).astype(held_as)


def setup_inputs(seed: int = 0) -> dict:
    arg_keys = jax.random.split(jax.random.key(seed), 12)
    crm_state = noise(arg_keys[0], (ROWS, NLON, CLEV, FIELDS * CRMCOL), 1.0, 4.0, ((0, 4), (1, 32)))
    gcm_state = noise(arg_keys[1], (ROWS, NLON, FIELDS, GLEV), 1.0, 4.0, ((0, 4), (1, 32)))
    micro_flags = set_ends((jax.random.randint(arg_keys[2], (ROWS, NLON), 0, 2) < 1).astype(jnp.int32), jax.random.fold_in(arg_keys[2], 1), 0, 1)
    load_plan = draw_load_plan(jax.random.fold_in(arg_keys[11], 71), 0)
    h_mix = noise(arg_keys[4], (CRMCOL, CRMCOL), CRMCOL ** -0.5, 0.75)
    v_mix = noise(arg_keys[5], (CLEV, CLEV), CLEV ** -0.5, 0.75)
    to_crm = noise(arg_keys[6], (CLEV, GLEV), GLEV ** -0.5, 0.75, (), jnp.float32)
    to_gcm = noise(arg_keys[7], (GLEV, CLEV), CLEV ** -0.5, 0.75, (), jnp.float32)
    polar_tracer = noise(arg_keys[8], (ROWS, GLEV, NLON), 1.0, 6.0, ((0, 4), (2, 32)), jnp.float32)
    courant_shift = draw_courant_shift(jax.random.fold_in(arg_keys[11], 71), 0)
    courant_frac = jnp.clip(1.0 * jax.random.uniform(arg_keys[10], (ROWS, GLEV), jnp.float32) ** level_of(arg_keys[10], (ROWS, GLEV), ((0, 4),), -0.2, 0.2), 0.0, 1.0)
    return dict(crm_state=crm_state, gcm_state=gcm_state, micro_flags=micro_flags, load_plan=load_plan, h_mix=h_mix, v_mix=v_mix, to_crm=to_crm, to_gcm=to_gcm, polar_tracer=polar_tracer, courant_shift=courant_shift, courant_frac=courant_frac)


def crm_advance(state_in, gcm_cols, flags, h_mix, v_mix, to_crm, to_gcm):
    count = state_in.shape[0]
    forcing = jnp.einsum("lg,nfg->nlf", to_crm, gcm_cols.astype(jnp.float32), precision=lax.Precision.HIGHEST)
    start = state_in.astype(jnp.float32).reshape(count, CLEV, FIELDS, CRMCOL)
    h_wide = h_mix.astype(jnp.float32)
    v_wide = v_mix.astype(jnp.float32)
    active = (flags == 1)[:, None, None]

    def substep(step, field_now):
        operand = field_now.astype(jnp.bfloat16).astype(jnp.float32)
        mixed = jnp.einsum("nlfc,cd->nlfd", operand, h_wide).astype(jnp.bfloat16).astype(jnp.float32)
        lifted = jnp.einsum("ml,nlfd->nmfd", v_wide, mixed)
        conversion = jnp.where(active, 0.5 * jnp.tanh(field_now[:, :, 0] * field_now[:, :, 1]), -0.25 * field_now[:, :, 0])
        adjust = jnp.concatenate([conversion[:, :, None], -conversion[:, :, None], jnp.zeros((count, CLEV, FIELDS - 2, CRMCOL), jnp.float32)], axis=2)
        return jnp.tanh(lifted) + 0.5 * forcing[..., None] + adjust

    final = lax.fori_loop(0, NSUB, substep, start)
    change = jnp.mean(final, axis=3) - jnp.mean(start, axis=3)
    tend = jnp.einsum("gl,nlf->nfg", to_gcm, change, precision=lax.Precision.HIGHEST)
    return final.astype(jnp.bfloat16).reshape(count, CLEV, FIELDS * CRMCOL), tend


def reference(crm_state, gcm_state, micro_flags, load_plan, h_mix, v_mix, to_crm, to_gcm, polar_tracer, courant_shift, courant_frac):
    def one_row(inputs):
        return crm_advance(inputs[0], inputs[1], inputs[2], h_mix, v_mix, to_crm, to_gcm)

    advanced, tendency = lax.map(one_row, (crm_state, gcm_state, micro_flags))
    row_ids = jnp.arange(ROWS, dtype=jnp.int32)[:, None] * jnp.ones((1, NLON), jnp.int32)
    new_state = jnp.zeros_like(advanced).at[row_ids, load_plan].set(advanced)
    updated = polar_tracer + jnp.transpose(tendency[:, :, 0, :], (0, 2, 1))
    cells = jnp.arange(NLON, dtype=jnp.int32)
    first = (cells[None, None, :] - courant_shift[:, :, None]) % NLON
    second = (first - 1) % NLON
    upwind = jnp.take_along_axis(updated, first.astype(jnp.int32), axis=2)
    beyond = jnp.take_along_axis(updated, second.astype(jnp.int32), axis=2)
    weight = courant_frac[:, :, None]
    polar_next = (1.0 - weight) * upwind + weight * beyond
    return new_state, tendency, polar_next
```

```python
import functools

import jax
import jax.numpy as jnp
from jax import lax
from jax.experimental import pallas as pl
from jax.experimental.pallas import tpu as pltpu
from jax.sharding import PartitionSpec as P

NSUB = 18
MESH = pl.DeviceIdType.MESH
F32 = jnp.float32
BF16 = jnp.bfloat16
HIGHEST = lax.Precision.HIGHEST

SIZES = (4, 4, 2)


def _hops(off):
    return sum(min(d, n - d) for d, n in zip(off, SIZES))


OFFSETS = sorted(
    ((a, b, c) for a in range(4) for b in range(4) for c in range(2)),
    key=lambda off: (-_hops(off), off),
)
NBLK = len(OFFSETS)
CHUNKS = 4
PER = NBLK // CHUNKS
COLS = 2 * PER


def _shifted(me, off):
    x, z, y = me // 8, (me // 2) % 4, me % 2
    return ((x + off[0]) % 4) * 8 + ((z + off[1]) % 4) * 2 + (y + off[2]) % 2


def _pick(index, values):
    out = jnp.int32(values[0])
    for i, value in enumerate(values[1:], 1):
        out = jnp.where(index == i, jnp.int32(value), out)
    return out


def _iota(shape, axis):
    return lax.broadcasted_iota(jnp.int32, shape, axis)


def _dot(a, b, **kw):
    return jnp.dot(a, b, preferred_element_type=F32, **kw)


def _onehot(mask):
    return jnp.where(mask, jnp.float32(1), jnp.float32(0)).astype(BF16)


def advance(
    order,
    plan_s,
    flags,
    plan_v,
    crm,
    gcm,
    h_ref,
    v_ref,
    to_crm,
    to_gcm,
    tracer,
    recv,
    trec,
    prec,
    tbuf,
    crm_v,
    xa,
    xb,
    s0,
    fa,
    fb,
    gsc,
    hbd,
    vbd,
    ea,
    eb,
    ra,
    rb,
    tc,
    tg,
    sq,
    trt,
    updf,
    usend,
    snd,
    in_sem,
    self_sem,
    ssem,
    rsem,
    pssem,
    prsem,
    tssem,
    trsem,
):
    me = lax.axis_index("lon")
    load = pltpu.make_async_copy(crm, crm_v, in_sem)
    load.start()

    peers = [_shifted(me, off) for off in OFFSETS]
    barrier = pltpu.get_barrier_semaphore()
    for k in range(NBLK - 1):
        pl.semaphore_signal(barrier, inc=1, device_id={"lon": peers[k]}, device_id_type=MESH)

    tile_h = _onehot(_iota((64, 256), 1) % 64 == _iota((64, 256), 0))
    tile_ht = _onehot(_iota((256, 64), 0) % 64 == _iota((256, 64), 1))
    tile_v = _onehot(_iota((58, 256), 1) % 64 == _iota((58, 256), 0))
    tile_vt = _onehot(_iota((256, 58), 0) % 64 == _iota((256, 58), 1))
    diag = _iota((256, 256), 0) // 64 == _iota((256, 256), 1) // 64
    h_rep = _dot(_dot(tile_ht, h_ref[...]).astype(BF16), tile_h)
    v_rep = _dot(_dot(tile_vt, v_ref[...]).astype(BF16), tile_v)
    hbd[...] = jnp.where(diag, h_rep, 0.0).astype(BF16)
    vbd[...] = jnp.where(diag, v_rep, 0.0).astype(BF16)
    k_row, j_col = _iota((256, 256), 0) % 128, _iota((256, 256), 1)
    ea[...] = _onehot(k_row == j_col // 64)
    eb[...] = _onehot(k_row == jnp.where(j_col < 128, 4 + j_col // 64, 10 + j_col // 64))
    r_row, r_col = _iota((256, 128), 0), _iota((256, 128), 1)
    part = jnp.float32(1.0 / 64)
    ra[...] = jnp.where(r_col == r_row // 64, part, 0.0).astype(BF16)
    rb[...] = jnp.where(
        r_col == jnp.where(r_row < 128, 4 + r_row // 64, 10 + r_row // 64), part, 0.0
    ).astype(BF16)
    tc[...] = jnp.zeros_like(tc)
    tc[0:58, 0:72] = 0.5 * to_crm[...]
    tg[...] = jnp.zeros_like(tg)
    tg[0:72, 0:58] = to_gcm[...]
    gsc[...] = jnp.zeros_like(gsc)
    xa[...] = jnp.zeros_like(xa)
    xb[...] = jnp.zeros_like(xb)
    s0[...] = jnp.zeros_like(s0)
    for r in range(2):
        sq[...] = jnp.zeros_like(sq)
        sq[0:72, 0:32] = tracer[r]
        trt[r] = jnp.transpose(sq[...])[0:32, :]

    load.wait()
    pl.semaphore_wait(barrier, NBLK - 1)

    def plan_copy(k):
        return pltpu.make_async_remote_copy(
            src_ref=plan_v,
            dst_ref=prec.at[me],
            send_sem=pssem.at[k],
            recv_sem=prsem.at[k],
            device_id={"lon": peers[k]},
            device_id_type=MESH,
        )

    for k in range(NBLK - 1):
        plan_copy(k).start()
    own_plan = pltpu.make_async_copy(plan_v, prec.at[me], pssem.at[NBLK - 1])
    own_plan.start()

    low = _iota((64, 128), 1) < 64
    sgn = jnp.where(_iota((1, 128), 1) < 64, jnp.float32(1), jnp.float32(-1))

    def state_copy(k, dest):
        return pltpu.make_async_remote_copy(
            src_ref=snd.at[k],
            dst_ref=recv.at[me],
            send_sem=ssem.at[k],
            recv_sem=rsem.at[k],
            device_id={"lon": dest},
            device_id_type=MESH,
        )

    def chunk(ch, carry):
        dests = []
        for j in range(PER):
            offs = [OFFSETS[c * PER + j] for c in range(CHUNKS)]
            off = [_pick(ch, [o[i] for o in offs]) for i in range(3)]
            dests.append(_shifted(me, off))
        picks = [(r, order[r, dests[j]]) for j in range(PER) for r in range(2)]
        avs, bvs = [], []
        for c, (r, i) in enumerate(picks):
            half = pl.ds((c % 2) * 128, 128)
            column = crm_v[r, i]
            xa[c, 0:58, :] = column[:, 0:256]
            xb[c // 2, 0:58, half] = column[:, 256:384]
            s0[c, 0:58, :] = column[:, 0:128].astype(F32)
            gsc[c * 8 : c * 8 + 6, 0:72] = gcm[r, i].astype(F32)
            flag = flags[r, i]
            avs.append(sgn * jnp.where(flag == 1, jnp.float32(0.5), jnp.float32(0)))
            bvs.append(sgn * jnp.where(flag == 1, jnp.float32(0), jnp.float32(-0.25)))
        forcing = lax.dot_general(
            tc[...],
            gsc[...],
            (((1,), (1,)), ((), ())),
            precision=HIGHEST,
            preferred_element_type=F32,
        )
        for c in range(COLS):
            turned = forcing if c == 0 else pltpu.roll(forcing, 128 - 8 * c, 1)
            hi = turned.astype(BF16)
            lo = (turned - hi.astype(F32)).astype(BF16)
            both = jnp.concatenate([hi, lo], axis=1)
            fa[c] = _dot(both, ea[...])
            if c % 2 == 0:
                fb[c // 2] = _dot(both, eb[...])

        def substep(step, carry):
            h, v = hbd[...], vbd[...]
            for q in range(COLS // 4):
                x = xa[4 * q : 4 * q + 4].reshape(256, 256)
                mixed = _dot(x, h).astype(BF16)
                grown = jnp.tanh(_dot(v, mixed))
                for i in range(4):
                    c = 4 * q + i
                    new = grown[64 * i : 64 * i + 64] + fa[c]
                    old = s0[c]
                    turned = pltpu.roll(old, 64, 1)
                    adjust = (
                        jnp.tanh(old * turned) * avs[c] + jnp.where(low, old, turned) * bvs[c]
                    )
                    first = new[:, 0:128] + adjust
                    s0[c] = first
                    xa[c, :, 0:128] = first.astype(BF16)
                    xa[c, :, 128:256] = new[:, 128:256].astype(BF16)
            for q in range(COLS // 8):
                x = xb[4 * q : 4 * q + 4].reshape(256, 256)
                mixed = _dot(x, h).astype(BF16)
                grown = jnp.tanh(_dot(v, mixed))
                for i in range(4):
                    c = 4 * q + i
                    xb[c] = (grown[64 * i : 64 * i + 64] + fb[c]).astype(BF16)
            return carry

        lax.fori_loop(0, NSUB, substep, 0)

        total = jnp.zeros((64, 128), F32)
        for c, (r, i) in enumerate(picks):
            half = pl.ds((c % 2) * 128, 128)
            k = ch * PER + c // 2
            begun = crm_v[r, i]
            done_a, done_b = xa[c, 0:58, :], xb[c // 2, 0:58, half]
            snd[k, r, :, 0:256] = done_a
            snd[k, r, :, 256:384] = done_b
            xa[c, 0:58, :] = (done_a.astype(F32) - begun[:, 0:256].astype(F32)).astype(BF16)
            xb[c // 2, 0:58, half] = (done_b.astype(F32) - begun[:, 256:384].astype(F32)).astype(
                BF16
            )
            mean = _dot(xa[c], ra[...])
            total += mean if c == 0 else pltpu.roll(mean, 8 * c, 1)
            if c % 2 == 1:
                mean = _dot(xb[c // 2], rb[...])
                total += mean if c == 1 else pltpu.roll(mean, 8 * (c - 1), 1)
        tend = jnp.transpose(_dot(tg[...], total, precision=HIGHEST))
        for c in range(COLS):
            tbuf[dests[c // 2], c % 2] = tend[8 * c : 8 * c + 8]

        for j in range(PER - 1):
            state_copy(ch * PER + j, dests[j]).start()

        @pl.when(ch < CHUNKS - 1)
        def _():
            state_copy(ch * PER + PER - 1, dests[PER - 1]).start()

        return carry

    lax.fori_loop(0, CHUNKS, chunk, 0)

    own_state = pltpu.make_async_copy(snd.at[NBLK - 1], recv.at[me], self_sem)
    own_state.start()

    def row(i, carry):
        for r in range(2):
            updf[r, pl.ds(i, 1), :] = tbuf[plan_s[r, i] // 32, r, 0:1, :]
        return carry

    lax.fori_loop(0, 32, row, 0, unroll=8)
    usend[...] = (updf[...] + trt[...]).astype(BF16)

    def tracer_copy(k):
        return pltpu.make_async_remote_copy(
            src_ref=usend,
            dst_ref=trec.at[me],
            send_sem=tssem.at[k],
            recv_sem=trsem.at[k],
            device_id={"lon": peers[k]},
            device_id_type=MESH,
        )

    for k in range(NBLK - 1):
        tracer_copy(k).start()
    own_tracer = pltpu.make_async_copy(usend, trec.at[me], tssem.at[NBLK - 1])
    own_tracer.start()
    own_state.wait()
    own_plan.wait()
    own_tracer.wait()
    for k in range(NBLK - 1):
        plan_copy(k).wait()
        state_copy(k, peers[k]).wait()
        tracer_copy(k).wait()


def place(
    plan_s,
    recv,
    trec,
    prec,
    tbuf,
    shift,
    frac,
    state_out,
    tend_out,
    polar_out,
    rbuf,
    slots_v,
    slots_s,
    cs,
    cf,
    sq,
    in_sem,
    slot_sem,
    out_sem,
):
    me = lax.axis_index("lon")
    loads = [pltpu.make_async_copy(recv.at[pl.ds(8 * q, 8)], rbuf.at[pl.ds(8 * q, 8)], in_sem.at[q]) for q in range(4)]
    for load in loads:
        load.start()
    plans = prec[...]
    mine = jnp.where(plans // 32 == me, plans % 32, 0)
    slots_v[...] = jnp.broadcast_to(jnp.sum(mine, axis=2, keepdims=True), (32, 2, 128))
    to_smem = pltpu.make_async_copy(slots_v, slots_s, slot_sem)
    to_smem.start()
    to_smem.wait()
    for q in range(4):
        loads[q].wait()
        for s in range(8 * q, 8 * q + 8):
            for r in range(2):
                pltpu.make_async_copy(
                    rbuf.at[s, r], state_out.at[r, slots_s[s, r, 0]], out_sem.at[2 * s + r]
                ).start()

    for r in range(2):
        for i in range(32):
            tend_out[r, i] = tbuf[plan_s[r, i] // 32, r, 0:6, 0:72]

    cs[...] = jnp.zeros_like(cs)
    cf[...] = jnp.zeros_like(cf)
    cs[0:2, 0:72] = shift[...]
    cf[0:2, 0:72] = frac[...]
    for r in range(2):
        base = (me * 32 - 1 - cs[r : r + 1, :]) & 1023
        whole = trec[:, r].astype(F32).reshape(1024, 128)
        cut = jnp.concatenate([whole[512:1024], whole[0:32]], axis=0)
        now = jnp.where((base & 512) != 0, cut, whole[0:544])
        for size in (256, 128, 64, 32, 16, 8):
            rows = size + 32
            now = jnp.where((base & size) != 0, now[size : size + rows], now[0:rows])
        for size in (4, 2, 1):
            now = jnp.where((base & size) != 0, pltpu.roll(now, 40 - size, 0), now)
        weight = cf[r : r + 1, :]
        result = (1.0 - weight) * pltpu.roll(now, 39, 0) + weight * now
        sq[...] = jnp.zeros_like(sq)
        sq[0:32, :] = result[0:32]
        polar_out[r] = jnp.transpose(sq[...])[0:72, 0:32]

    for s in range(32):
        for r in range(2):
            pltpu.make_async_copy(
                rbuf.at[s, r], state_out.at[r, slots_s[s, r, 0]], out_sem.at[2 * s + r]
            ).wait()


def per_device(
    crm_state,
    gcm_state,
    micro_flags,
    load_plan,
    h_mix,
    v_mix,
    to_crm,
    to_gcm,
    polar_tracer,
    courant_shift,
    courant_frac,
):
    owners = load_plan // 32
    spots = jnp.arange(32, dtype=jnp.int32)
    order = jnp.sum(
        jnp.where(owners[:, None, :] == spots[None, :, None], spots[None, None, :], 0), axis=2
    )
    smem = pl.BlockSpec(memory_space=pltpu.SMEM)
    vmem = pl.BlockSpec(memory_space=pltpu.VMEM)
    hbm = pl.BlockSpec(memory_space=pl.ANY)
    recv, trec, prec, tbuf = pl.pallas_call(
        advance,
        out_shape=(
            jax.ShapeDtypeStruct((32, 2, 58, 384), BF16),
            jax.ShapeDtypeStruct((32, 2, 32, 128), BF16),
            jax.ShapeDtypeStruct((32, 2, 32), jnp.int32),
            jax.ShapeDtypeStruct((32, 2, 8, 128), F32),
        ),
        in_specs=[smem, smem, smem, vmem, hbm] + [vmem] * 6,
        out_specs=(hbm, hbm, hbm, vmem),
        scratch_shapes=[
            pltpu.VMEM((2, 32, 58, 384), BF16),
            pltpu.VMEM((COLS, 64, 256), BF16),
            pltpu.VMEM((COLS // 2, 64, 256), BF16),
            pltpu.VMEM((COLS, 64, 128), F32),
            pltpu.VMEM((COLS, 64, 256), F32),
            pltpu.VMEM((COLS // 2, 64, 256), F32),
            pltpu.VMEM((128, 128), F32),
            pltpu.VMEM((256, 256), BF16),
            pltpu.VMEM((256, 256), BF16),
            pltpu.VMEM((256, 256), BF16),
            pltpu.VMEM((256, 256), BF16),
            pltpu.VMEM((256, 128), BF16),
            pltpu.VMEM((256, 128), BF16),
            pltpu.VMEM((64, 128), F32),
            pltpu.VMEM((128, 64), F32),
            pltpu.VMEM((128, 128), F32),
            pltpu.VMEM((2, 32, 128), F32),
            pltpu.VMEM((2, 32, 128), F32),
            pltpu.VMEM((2, 32, 128), BF16),
            pltpu.VMEM((32, 2, 58, 384), BF16),
            pltpu.SemaphoreType.DMA,
            pltpu.SemaphoreType.DMA,
            pltpu.SemaphoreType.DMA((NBLK,)),
            pltpu.SemaphoreType.DMA((NBLK,)),
            pltpu.SemaphoreType.DMA((NBLK,)),
            pltpu.SemaphoreType.DMA((NBLK,)),
            pltpu.SemaphoreType.DMA((NBLK,)),
            pltpu.SemaphoreType.DMA((NBLK,)),
        ],
        compiler_params=pltpu.CompilerParams(collective_id=0, has_side_effects=True),
        name="advance",
    )(
        order,
        load_plan,
        micro_flags,
        load_plan,
        crm_state,
        gcm_state,
        h_mix,
        v_mix,
        to_crm,
        to_gcm,
        polar_tracer,
    )
    return pl.pallas_call(
        place,
        out_shape=(
            jax.ShapeDtypeStruct((2, 32, 58, 384), BF16),
            jax.ShapeDtypeStruct((2, 32, 6, 72), F32),
            jax.ShapeDtypeStruct((2, 72, 32), F32),
        ),
        in_specs=[smem, hbm] + [vmem] * 5,
        out_specs=(hbm, vmem, vmem),
        scratch_shapes=[
            pltpu.VMEM((32, 2, 58, 384), BF16),
            pltpu.VMEM((32, 2, 128), jnp.int32),
            pltpu.SMEM((32, 2, 128), jnp.int32),
            pltpu.VMEM((8, 128), jnp.int32),
            pltpu.VMEM((8, 128), F32),
            pltpu.VMEM((128, 128), F32),
            pltpu.SemaphoreType.DMA((4,)),
            pltpu.SemaphoreType.DMA,
            pltpu.SemaphoreType.DMA((64,)),
        ],
        name="place",
    )(load_plan, recv, trec, prec, tbuf, courant_shift, courant_frac)


def solution(mesh):
    in_specs = (
        P("lat", "lon", None, None),
        P("lat", "lon", None, None),
        P("lat", "lon"),
        P("lat", "lon"),
        P(),
        P(),
        P(),
        P(),
        P("lat", None, "lon"),
        P("lat", None),
        P("lat", None),
    )
    out_specs = (P("lat", "lon", None, None), P("lat", "lon", None, None), P("lat", None, "lon"))
    return jax.shard_map(
        per_device, mesh=mesh, in_specs=in_specs, out_specs=out_specs, check_vma=False
    )
```

```python
import functools

import jax
import jax.numpy as jnp
from jax import lax
from jax.experimental import pallas as pl
from jax.experimental.pallas import tpu as pltpu
from jax.sharding import PartitionSpec as P

NSUB = 18
MESH = pl.DeviceIdType.MESH
F32 = jnp.float32
BF16 = jnp.bfloat16
HIGHEST = lax.Precision.HIGHEST

SIZES = (4, 4, 2)


def _hops(off):
    return sum(min(d, n - d) for d, n in zip(off, SIZES))


OFFSETS = sorted(
    ((a, b, c) for a in range(4) for b in range(4) for c in range(2)),
    key=lambda off: (-_hops(off), off),
)
NBLK = len(OFFSETS)
CHUNKS = 4
PER = NBLK // CHUNKS
GROUPS = ((0, 8, 1, 9), (2, 3, 10, 11), (4, 5, 12, 13))
UNROLL = 3
MERGE = 3
STEP = 33


def _shifted(me, off):
    x, z, y = me // 8, (me // 2) % 4, me % 2
    return ((x + off[0]) % 4) * 8 + ((z + off[1]) % 4) * 2 + (y + off[2]) % 2


def _pick(index, values):
    out = jnp.int32(values[0])
    for i, value in enumerate(values[1:], 1):
        out = jnp.where(index == i, jnp.int32(value), out)
    return out


def _iota(shape, axis):
    return lax.broadcasted_iota(jnp.int32, shape, axis)


def _dot(a, b, **kw):
    return jnp.dot(a, b, preferred_element_type=F32, **kw)


def _onehot(mask):
    return jnp.where(mask, jnp.float32(1), jnp.float32(0)).astype(BF16)


def _lane_map(quarter, lanes):
    out = jnp.full(quarter.shape, lanes[0], jnp.int32)
    for i, lane in enumerate(lanes[1:], 1):
        out = jnp.where(quarter == i, lane, out)
    return out


def advance(
    plan_s,
    flags,
    plan_v,
    crm,
    gcm,
    h_ref,
    v_ref,
    to_crm,
    to_gcm,
    tracer,
    recv,
    trec,
    prec,
    tbuf,
    crm_v,
    cn,
    xs,
    x0,
    s0,
    fs,
    lf,
    gn,
    gsc,
    hbd,
    vbd,
    spread,
    gather,
    tc,
    tg,
    trt,
    updf,
    usend,
    snd,
    order_v,
    order,
    in_sem,
    order_sem,
    self_sem,
    ssem,
    rsem,
    pssem,
    prsem,
    tssem,
    trsem,
):
    me = lax.axis_index("lon")
    loads = [pltpu.make_async_copy(crm.at[r], crm_v.at[r], in_sem.at[r]) for r in range(2)]
    for load in loads:
        load.start()

    peers = [_shifted(me, off) for off in OFFSETS]
    barrier = pltpu.get_barrier_semaphore()
    for k in range(NBLK - 1):
        pl.semaphore_signal(barrier, inc=1, device_id={"lon": peers[k]}, device_id_type=MESH)

    for r in range(2):
        owners = jnp.broadcast_to(plan_v[r : r + 1, :] // 32, (32, 32))
        at = jnp.where(owners == _iota((32, 32), 0), _iota((32, 32), 1), 0)
        order_v[r] = jnp.broadcast_to(jnp.max(at, axis=1, keepdims=True), (32, 128))
    to_smem = pltpu.make_async_copy(order_v, order, order_sem)
    to_smem.start()

    tile_h = _onehot(_iota((64, 256), 1) % 64 == _iota((64, 256), 0))
    tile_ht = _onehot(_iota((256, 64), 0) % 64 == _iota((256, 64), 1))
    tile_v = _onehot(_iota((58, 256), 1) % 64 == _iota((58, 256), 0))
    tile_vt = _onehot(_iota((256, 58), 0) % 64 == _iota((256, 58), 1))
    diag = _iota((256, 256), 0) // 64 == _iota((256, 256), 1) // 64
    h_rep = _dot(_dot(tile_ht, h_ref[...]).astype(BF16), tile_h)
    v_rep = _dot(_dot(tile_vt, v_ref[...]).astype(BF16), tile_v)
    hbd[...] = jnp.where(diag, h_rep, 0.0).astype(BF16)
    vbd[...] = jnp.where(diag, v_rep, 0.0).astype(BF16)
    for t, lanes in enumerate(GROUPS):
        spread[t] = _onehot(_iota((256, 256), 0) % 128 == _lane_map(_iota((256, 256), 1) // 64, lanes))
        hit = _iota((256, 128), 1) == _lane_map(_iota((256, 128), 0) // 64, lanes)
        gather[t * 256 : t * 256 + 256, :] = jnp.where(hit, jnp.float32(1.0 / 64), 0.0).astype(BF16)
    tc[...] = jnp.zeros_like(tc)
    tc[0:58, 0:72] = 0.5 * to_crm[...]
    tg[...] = jnp.zeros_like(tg)
    tg[0:58, 0:72] = to_gcm[...]
    gsc[...] = jnp.zeros_like(gsc)
    gn[...] = jnp.zeros_like(gn)
    xs[...] = jnp.zeros_like(xs)
    x0[...] = jnp.zeros_like(x0)
    s0[...] = jnp.zeros_like(s0)
    trt[...] = jnp.zeros_like(trt)
    for r in range(2):
        trt[r, :, 0:72] = tracer[r]
        for f in range(6):
            gn[(r * 6 + f) * STEP : (r * 6 + f) * STEP + 32, 0:72] = gcm[r, f].astype(F32)

    for r in range(2):
        loads[r].wait()

        def widen(level, carry):
            block = crm_v[r, level].astype(F32)
            for t in range(3):
                cn[t, pl.ds((r * 58 + level) * STEP, 32), :] = block[:, 128 * t : 128 * t + 128]
            return carry

        lax.fori_loop(0, 58, widen, 0, unroll=2)
    to_smem.wait()
    pl.semaphore_wait(barrier, NBLK - 1)

    def plan_copy(k):
        return pltpu.make_async_remote_copy(
            src_ref=plan_v,
            dst_ref=prec.at[me],
            send_sem=pssem.at[k],
            recv_sem=prsem.at[k],
            device_id={"lon": peers[k]},
            device_id_type=MESH,
        )

    for k in range(NBLK - 1):
        plan_copy(k).start()
    own_plan = pltpu.make_async_copy(plan_v, prec.at[me], pssem.at[NBLK - 1])
    own_plan.start()

    low58 = _iota((58, 128), 1) < 64
    low64 = _iota((64, 128), 1) < 64
    low1 = _iota((1, 128), 1) < 64

    def state_copy(k, dest):
        return pltpu.make_async_remote_copy(
            src_ref=snd.at[k],
            dst_ref=recv.at[me],
            send_sem=ssem.at[k],
            recv_sem=rsem.at[k],
            device_id={"lon": dest},
            device_id_type=MESH,
        )

    def chunk(ch, carry):
        dests = []
        for j in range(PER):
            offs = [OFFSETS[c * PER + j] for c in range(CHUNKS)]
            off = [_pick(ch, [o[i] for o in offs]) for i in range(3)]
            dests.append(_shifted(me, off))
        avs, bvs = [], []
        for p in range(PER):
            cols, a, b = [], [], []
            for r in range(2):
                i = order[r, dests[p], 0]
                cols.append([cn[t, pl.ds(r * 58 * STEP + i, 58, stride=STEP), :] for t in range(3)])
                row = 16 * p + 8 * r
                gsc[row : row + 6, :] = gn[pl.ds(r * 6 * STEP + i, 6, stride=STEP), :]
                flag = flags[r, i]
                a.append(jnp.where(flag == 1, jnp.float32(0.5), jnp.float32(0)))
                b.append(jnp.where(flag == 1, jnp.float32(0), jnp.float32(-0.25)))
            avs.append(jnp.where(low1, a[0], a[1]))
            bvs.append(jnp.where(low1, b[0], b[1]))
            one, two = cols[0][0], cols[1][0]
            first = jnp.where(low58, one, pltpu.roll(two, 64, 1))
            second = jnp.where(low58, pltpu.roll(one, 64, 1), two)
            s0[p, 0:58, 0:128] = first
            s0[p, 0:58, 128:256] = second
            blocks = ((first, second), (cols[0][1], cols[1][1]), (cols[0][2], cols[1][2]))
            for t in range(3):
                for half in range(2):
                    narrow = blocks[t][half].astype(BF16)
                    xs[t * PER + p, 0:58, 128 * half : 128 * half + 128] = narrow
                    x0[t * PER + p, 0:58, 128 * half : 128 * half + 128] = narrow
        forcing = lax.dot_general(
            tc[...],
            gsc[...],
            (((1,), (1,)), ((), ())),
            precision=HIGHEST,
            preferred_element_type=F32,
        )
        for p in range(PER):
            turned = forcing if p == 0 else pltpu.roll(forcing, 128 - 16 * p, 1)
            hi = turned.astype(BF16)
            lf[p, :, 0:128] = hi
            lf[p, :, 128:256] = (turned - hi.astype(F32)).astype(BF16)
        both = lf[...].reshape(PER * 64, 256)
        for t in range(3):
            fs[t * PER : t * PER + PER] = _dot(both, spread[t]).reshape(PER, 64, 256)

        def substep(step, carry):
            h, v = hbd[...], vbd[...]
            for m in range(0, 3 * PER // 4, MERGE):
                x = xs[4 * m : 4 * (m + MERGE)].reshape(MERGE * 256, 256)
                all_mixed = _dot(x, h).astype(BF16)
                for q in range(m, m + MERGE):
                    mixed = all_mixed[256 * (q - m) : 256 * (q - m) + 256]
                    grown = jnp.tanh(_dot(v, mixed))
                    for i in range(4):
                        c = 4 * q + i
                        new = grown[64 * i : 64 * i + 64] + fs[c]
                        if c < PER:
                            one, two = s0[c, :, 0:128], s0[c, :, 128:256]
                            adjust = jnp.tanh(one * two) * avs[c] + one * bvs[c]
                            first, second = new[:, 0:128] + adjust, new[:, 128:256] - adjust
                            s0[c, :, 0:128] = first
                            s0[c, :, 128:256] = second
                            xs[c, :, 0:128] = first.astype(BF16)
                            xs[c, :, 128:256] = second.astype(BF16)
                        else:
                            xs[c] = new.astype(BF16)
            return carry

        lax.fori_loop(0, NSUB, substep, 0, unroll=UNROLL)

        for p in range(PER):
            k = ch * PER + p
            one, two = s0[p, :, 0:128], s0[p, :, 128:256]
            left = jnp.where(low64, one, pltpu.roll(two, 64, 1)).astype(BF16)
            right = jnp.where(low64, pltpu.roll(one, 64, 1), two).astype(BF16)
            snd[k, 0, :, 0:128] = left[0:58]
            snd[k, 1, :, 0:128] = right[0:58]
            for t in (1, 2):
                for r in range(2):
                    snd[k, r, :, 128 * t : 128 * t + 128] = xs[
                        t * PER + p, 0:58, 128 * r : 128 * r + 128
                    ]
        mean = jnp.zeros((PER * 64, 128), F32)
        for t in range(3):
            diff = (xs[t * PER : t * PER + PER] - x0[t * PER : t * PER + PER]).reshape(PER * 64, 256)
            mean += _dot(diff, gather[t * 256 : t * 256 + 256, :])
        total = mean[0:64]
        for p in range(1, PER):
            total += pltpu.roll(mean[64 * p : 64 * p + 64], 16 * p, 1)
        tend = _dot(jnp.transpose(total), tg[...], precision=HIGHEST)
        for p in range(PER):
            for r in range(2):
                row = 16 * p + 8 * r
                tbuf[dests[p], r] = tend[row : row + 8]

        for j in range(PER - 1):
            state_copy(ch * PER + j, dests[j]).start()

        @pl.when(ch < CHUNKS - 1)
        def _():
            state_copy(ch * PER + PER - 1, dests[PER - 1]).start()

        return carry

    lax.fori_loop(0, CHUNKS, chunk, 0)

    own_state = pltpu.make_async_copy(snd.at[NBLK - 1], recv.at[me], self_sem)
    own_state.start()

    def row(i, carry):
        for r in range(2):
            updf[r, pl.ds(i, 1), :] = tbuf[plan_s[r, i] // 32, r, 0:1, :]
        return carry

    lax.fori_loop(0, 32, row, 0, unroll=8)
    usend[...] = (updf[...] + trt[...]).astype(BF16)

    def tracer_copy(k):
        return pltpu.make_async_remote_copy(
            src_ref=usend,
            dst_ref=trec.at[me],
            send_sem=tssem.at[k],
            recv_sem=trsem.at[k],
            device_id={"lon": peers[k]},
            device_id_type=MESH,
        )

    for k in range(NBLK - 1):
        tracer_copy(k).start()
    own_tracer = pltpu.make_async_copy(usend, trec.at[me], tssem.at[NBLK - 1])
    own_tracer.start()
    own_state.wait()
    own_plan.wait()
    own_tracer.wait()
    for k in range(NBLK - 1):
        plan_copy(k).wait()
        state_copy(k, peers[k]).wait()
        tracer_copy(k).wait()


def place(
    plan_s,
    recv,
    trec,
    prec,
    tbuf,
    shift,
    frac,
    state_out,
    tend_out,
    polar_out,
    rbuf,
    wide,
    obuf,
    tn,
    slots_v,
    slots_s,
    cs,
    cf,
    in_sem,
    slot_sem,
    out_sem,
):
    me = lax.axis_index("lon")
    loads = [
        pltpu.make_async_copy(recv.at[pl.ds(8 * q, 8)], rbuf.at[pl.ds(8 * q, 8)], in_sem.at[q])
        for q in range(4)
    ]
    for load in loads:
        load.start()
    plans = prec[...]
    mine = jnp.where(plans // 32 == me, plans % 32, 0)
    slots_v[...] = jnp.broadcast_to(jnp.max(mine, axis=2, keepdims=True), (32, 2, 128))
    to_smem = pltpu.make_async_copy(slots_v, slots_s, slot_sem)
    to_smem.start()

    for r in range(2):
        for i in range(32):
            tn[pl.ds(r * 6 * STEP + i, 6, stride=STEP), :] = tbuf[plan_s[r, i] // 32, r, 0:6, :]
        for f in range(6):
            at = (r * 6 + f) * STEP
            tend_out[r, f] = tn[at : at + 32, 0:72]

    cs[...] = jnp.zeros_like(cs)
    cf[...] = jnp.zeros_like(cf)
    cs[0:2, 0:72] = shift[...]
    cf[0:2, 0:72] = frac[...]
    for r in range(2):
        base = (me * 32 - 1 - cs[r : r + 1, :]) & 1023
        whole = trec[:, r].astype(F32).reshape(1024, 128)
        cut = jnp.concatenate([whole[512:1024], whole[0:32]], axis=0)
        now = jnp.where((base & 512) != 0, cut, whole[0:544])
        for size in (256, 128, 64, 32, 16, 8):
            rows = size + 32
            now = jnp.where((base & size) != 0, now[size : size + rows], now[0:rows])
        for size in (4, 2, 1):
            now = jnp.where((base & size) != 0, pltpu.roll(now, 40 - size, 0), now)
        weight = cf[r : r + 1, :]
        result = (1.0 - weight) * pltpu.roll(now, 39, 0) + weight * now
        polar_out[r] = result[0:32, 0:72]

    to_smem.wait()
    for q in range(4):
        loads[q].wait()

        def spot(s, carry):
            for r in range(2):
                column = rbuf[s, r].astype(F32)
                at = pl.ds(r * 58 * STEP + slots_s[s, r, 0], 58, stride=STEP)
                for t in range(3):
                    wide[t, at, :] = column[:, 128 * t : 128 * t + 128]
            return carry

        lax.fori_loop(8 * q, 8 * q + 8, spot, 0, unroll=2)

    outs = []
    for r in range(2):
        for part in range(2):

            def narrow(level, carry):
                for t in range(3):
                    obuf[r, level, :, 128 * t : 128 * t + 128] = wide[
                        t, pl.ds((r * 58 + level) * STEP, 32), :
                    ].astype(BF16)
                return carry

            lax.fori_loop(29 * part, 29 * part + 29, narrow, 0, unroll=True)
            piece = pl.ds(29 * part, 29)
            outs.append(
                pltpu.make_async_copy(
                    obuf.at[r, piece], state_out.at[r, piece], out_sem.at[2 * r + part]
                )
            )
            outs[-1].start()
    for out in outs:
        out.wait()


def per_device(
    crm_state,
    gcm_state,
    micro_flags,
    load_plan,
    h_mix,
    v_mix,
    to_crm,
    to_gcm,
    polar_tracer,
    courant_shift,
    courant_frac,
):
    smem = pl.BlockSpec(memory_space=pltpu.SMEM)
    vmem = pl.BlockSpec(memory_space=pltpu.VMEM)
    hbm = pl.BlockSpec(memory_space=pl.ANY)
    dma = pltpu.SemaphoreType.DMA
    recv, trec, prec, tbuf = pl.pallas_call(
        advance,
        out_shape=(
            jax.ShapeDtypeStruct((32, 2, 58, 384), BF16),
            jax.ShapeDtypeStruct((32, 2, 32, 128), BF16),
            jax.ShapeDtypeStruct((32, 2, 32), jnp.int32),
            jax.ShapeDtypeStruct((32, 2, 8, 128), F32),
        ),
        in_specs=[smem, smem, vmem, hbm] + [vmem] * 6,
        out_specs=(hbm, hbm, hbm, vmem),
        scratch_shapes=[
            pltpu.VMEM((2, 58, 32, 384), BF16),
            pltpu.VMEM((3, 2 * 58 * STEP, 128), F32),
            pltpu.VMEM((3 * PER, 64, 256), BF16),
            pltpu.VMEM((3 * PER, 64, 256), BF16),
            pltpu.VMEM((PER, 64, 256), F32),
            pltpu.VMEM((3 * PER, 64, 256), F32),
            pltpu.VMEM((PER, 64, 256), BF16),
            pltpu.VMEM((2 * 6 * STEP, 128), F32),
            pltpu.VMEM((128, 128), F32),
            pltpu.VMEM((256, 256), BF16),
            pltpu.VMEM((256, 256), BF16),
            pltpu.VMEM((3, 256, 256), BF16),
            pltpu.VMEM((768, 128), BF16),
            pltpu.VMEM((64, 128), F32),
            pltpu.VMEM((64, 128), F32),
            pltpu.VMEM((2, 32, 128), F32),
            pltpu.VMEM((2, 32, 128), F32),
            pltpu.VMEM((2, 32, 128), BF16),
            pltpu.VMEM((32, 2, 58, 384), BF16),
            pltpu.VMEM((2, 32, 128), jnp.int32),
            pltpu.SMEM((2, 32, 128), jnp.int32),
            dma((2,)),
            dma,
            dma,
            dma((NBLK,)),
            dma((NBLK,)),
            dma((NBLK,)),
            dma((NBLK,)),
            dma((NBLK,)),
            dma((NBLK,)),
        ],
        compiler_params=pltpu.CompilerParams(collective_id=0, has_side_effects=True),
        name="advance",
    )(
        load_plan,
        micro_flags,
        load_plan,
        jnp.transpose(crm_state, (0, 2, 1, 3)),
        jnp.transpose(gcm_state, (0, 2, 1, 3)),
        h_mix,
        v_mix,
        to_crm,
        to_gcm.T,
        jnp.transpose(polar_tracer, (0, 2, 1)),
    )
    new_state, tendency, polar_next = pl.pallas_call(
        place,
        out_shape=(
            jax.ShapeDtypeStruct((2, 58, 32, 384), BF16),
            jax.ShapeDtypeStruct((2, 6, 32, 72), F32),
            jax.ShapeDtypeStruct((2, 32, 72), F32),
        ),
        in_specs=[smem, hbm] + [vmem] * 5,
        out_specs=(hbm, vmem, vmem),
        scratch_shapes=[
            pltpu.VMEM((32, 2, 58, 384), BF16),
            pltpu.VMEM((3, 2 * 58 * STEP, 128), F32),
            pltpu.VMEM((2, 58, 32, 384), BF16),
            pltpu.VMEM((2 * 6 * STEP, 128), F32),
            pltpu.VMEM((32, 2, 128), jnp.int32),
            pltpu.SMEM((32, 2, 128), jnp.int32),
            pltpu.VMEM((8, 128), jnp.int32),
            pltpu.VMEM((8, 128), F32),
            dma((4,)),
            dma,
            dma((4,)),
        ],
        name="place",
    )(load_plan, recv, trec, prec, tbuf, courant_shift, courant_frac)
    return (
        jnp.transpose(new_state, (0, 2, 1, 3)),
        jnp.transpose(tendency, (0, 2, 1, 3)),
        jnp.transpose(polar_next, (0, 2, 1)),
    )


def solution(mesh):
    in_specs = (
        P("lat", "lon", None, None),
        P("lat", "lon", None, None),
        P("lat", "lon"),
        P("lat", "lon"),
        P(),
        P(),
        P(),
        P(),
        P("lat", None, "lon"),
        P("lat", None),
        P("lat", None),
    )
    out_specs = (P("lat", "lon", None, None), P("lat", "lon", None, None), P("lat", None, "lon"))
    return jax.shard_map(
        per_device, mesh=mesh, in_specs=in_specs, out_specs=out_specs, check_vma=False
    )
```

```python
import functools

import jax
import jax.numpy as jnp
from jax import lax
from jax.experimental import pallas as pl
from jax.experimental.pallas import tpu as pltpu
from jax.sharding import PartitionSpec as P

NSUB = 18
MESH = pl.DeviceIdType.MESH
F32 = jnp.float32
BF16 = jnp.bfloat16
HIGHEST = lax.Precision.HIGHEST

SIZES = (4, 4, 2)


def _hops(off):
    return sum(min(d, n - d) for d, n in zip(off, SIZES))


OFFSETS = sorted(
    ((a, b, c) for a in range(4) for b in range(4) for c in range(2)),
    key=lambda off: (-_hops(off), off),
)
NBLK = len(OFFSETS)
CHUNKS = 4
PER = NBLK // CHUNKS
GROUPS = ((0, 8, 1, 9), (2, 3, 10, 11), (4, 5, 12, 13))
UNROLL = 18
MERGE = 3
STEP = 33


def _shifted(me, off):
    x, z, y = me // 8, (me // 2) % 4, me % 2
    return ((x + off[0]) % 4) * 8 + ((z + off[1]) % 4) * 2 + (y + off[2]) % 2


def _pick(index, values):
    out = jnp.int32(values[0])
    for i, value in enumerate(values[1:], 1):
        out = jnp.where(index == i, jnp.int32(value), out)
    return out


def _iota(shape, axis):
    return lax.broadcasted_iota(jnp.int32, shape, axis)


def _dot(a, b, **kw):
    return jnp.dot(a, b, preferred_element_type=F32, **kw)


def _onehot(mask):
    return jnp.where(mask, jnp.float32(1), jnp.float32(0)).astype(BF16)


def _lane_map(quarter, lanes):
    out = jnp.full(quarter.shape, lanes[0], jnp.int32)
    for i, lane in enumerate(lanes[1:], 1):
        out = jnp.where(quarter == i, lane, out)
    return out


def advance(
    flags,
    plan_v,
    crm,
    gcm,
    h_ref,
    v_ref,
    to_crm,
    to_gcm,
    tracer,
    recv,
    trec,
    prec,
    tbuf,
    crm_v,
    cn,
    xs,
    x0,
    s0,
    fs,
    lf,
    gn,
    gsc,
    hbd,
    vbd,
    spread,
    gather,
    tc,
    tg,
    trt,
    updf,
    usend,
    snd,
    pack,
    order_v,
    order,
    in_sem,
    order_sem,
    self_sem,
    ssem,
    rsem,
    pssem,
    prsem,
    tssem,
    trsem,
):
    me = lax.axis_index("lon")
    loads = [pltpu.make_async_copy(crm.at[r], crm_v.at[r], in_sem.at[r]) for r in range(2)]
    for load in loads:
        load.start()

    peers = [_shifted(me, off) for off in OFFSETS]
    barrier = pltpu.get_barrier_semaphore()
    for k in range(NBLK - 1):
        pl.semaphore_signal(barrier, inc=1, device_id={"lon": peers[k]}, device_id_type=MESH)

    for r in range(2):
        owners = jnp.broadcast_to(plan_v[r : r + 1, :] // 32, (32, 32))
        at = jnp.where(owners == _iota((32, 32), 0), _iota((32, 32), 1), 0)
        order_v[r] = jnp.broadcast_to(jnp.max(at, axis=1, keepdims=True), (32, 128))
    lane = _iota((1, 128), 1)
    bound = jnp.full((1, 128), 64, jnp.int32)
    for k in range(NBLK):
        bound = jnp.where(lane // 2 == k, peers[k], bound)
    value = jnp.where(_iota((32, 128), 1) % 2 == 0, order_v[0], order_v[1] + 32)
    spot = jnp.where(bound == _iota((32, 128), 0), value, 0)
    pack[...] = jnp.zeros_like(pack)
    pack[0:2, 0:32] = plan_v[...]
    pack[2:3, :] = jnp.max(spot, axis=0, keepdims=True)
    to_smem = pltpu.make_async_copy(order_v, order, order_sem)
    to_smem.start()

    tile_h = _onehot(_iota((64, 256), 1) % 64 == _iota((64, 256), 0))
    tile_ht = _onehot(_iota((256, 64), 0) % 64 == _iota((256, 64), 1))
    tile_v = _onehot(_iota((58, 256), 1) % 64 == _iota((58, 256), 0))
    tile_vt = _onehot(_iota((256, 58), 0) % 64 == _iota((256, 58), 1))
    diag = _iota((256, 256), 0) // 64 == _iota((256, 256), 1) // 64
    h_rep = _dot(_dot(tile_ht, h_ref[...]).astype(BF16), tile_h)
    v_rep = _dot(_dot(tile_vt, v_ref[...]).astype(BF16), tile_v)
    hbd[...] = jnp.where(diag, h_rep, 0.0).astype(BF16)
    vbd[...] = jnp.where(diag, v_rep, 0.0).astype(BF16)
    for t, lanes in enumerate(GROUPS):
        spread[t] = _onehot(_iota((256, 256), 0) % 128 == _lane_map(_iota((256, 256), 1) // 64, lanes))
        hit = _iota((256, 128), 1) == _lane_map(_iota((256, 128), 0) // 64, lanes)
        gather[t * 256 : t * 256 + 256, :] = jnp.where(hit, jnp.float32(1.0 / 64), 0.0).astype(BF16)
    tc[...] = jnp.zeros_like(tc)
    tc[0:58, 0:72] = 0.5 * to_crm[...]
    tg[...] = jnp.zeros_like(tg)
    tg[0:58, 0:72] = to_gcm[...]
    gsc[...] = jnp.zeros_like(gsc)
    gn[...] = jnp.zeros_like(gn)
    xs[...] = jnp.zeros_like(xs)
    x0[...] = jnp.zeros_like(x0)
    s0[...] = jnp.zeros_like(s0)
    trt[...] = jnp.zeros_like(trt)
    for r in range(2):
        trt[r, :, 0:72] = tracer[r]
        for f in range(6):
            gn[(r * 6 + f) * STEP : (r * 6 + f) * STEP + 32, 0:72] = gcm[r, f].astype(F32)

    for r in range(2):
        loads[r].wait()

        def widen(level, carry):
            block = crm_v[r, level].astype(F32)
            for t in range(3):
                cn[t, pl.ds((r * 58 + level) * STEP, 32), :] = block[:, 128 * t : 128 * t + 128]
            return carry

        lax.fori_loop(0, 58, widen, 0, unroll=2)
    to_smem.wait()

    def pack_copy(k):
        return pltpu.make_async_remote_copy(
            src_ref=pack,
            dst_ref=prec.at[me],
            send_sem=pssem.at[k],
            recv_sem=prsem.at[k],
            device_id={"lon": peers[k]},
            device_id_type=MESH,
        )

    own_pack = pltpu.make_async_copy(pack, prec.at[me], pssem.at[NBLK - 1])
    own_pack.start()

    def tracer_copy(ch, k):
        return pltpu.make_async_remote_copy(
            src_ref=usend.at[ch],
            dst_ref=trec.at[me, ch],
            send_sem=tssem.at[ch, k],
            recv_sem=trsem.at[ch, k],
            device_id={"lon": peers[k]},
            device_id_type=MESH,
        )

    def own_tracer(ch):
        return pltpu.make_async_copy(usend.at[ch], trec.at[me, ch], tssem.at[ch, NBLK - 1])

    low58 = _iota((58, 128), 1) < 64
    low64 = _iota((64, 128), 1) < 64
    low1 = _iota((1, 128), 1) < 64

    def state_copy(k, dest):
        return pltpu.make_async_remote_copy(
            src_ref=snd.at[k],
            dst_ref=recv.at[me],
            send_sem=ssem.at[k],
            recv_sem=rsem.at[k],
            device_id={"lon": dest},
            device_id_type=MESH,
        )

    def chunk(ch, carry):
        dests = []
        for j in range(PER):
            offs = [OFFSETS[c * PER + j] for c in range(CHUNKS)]
            off = [_pick(ch, [o[i] for o in offs]) for i in range(3)]
            dests.append(_shifted(me, off))
        avs, bvs = [], []
        for p in range(PER):
            cols, a, b = [], [], []
            for r in range(2):
                i = order[r, dests[p], 0]
                cols.append([cn[t, pl.ds(r * 58 * STEP + i, 58, stride=STEP), :] for t in range(3)])
                row = 16 * p + 8 * r
                gsc[row : row + 6, :] = gn[pl.ds(r * 6 * STEP + i, 6, stride=STEP), :]
                flag = flags[r, i]
                a.append(jnp.where(flag == 1, jnp.float32(0.5), jnp.float32(0)))
                b.append(jnp.where(flag == 1, jnp.float32(0), jnp.float32(-0.25)))
            avs.append(jnp.where(low1, a[0], a[1]))
            bvs.append(jnp.where(low1, b[0], b[1]))
            one, two = cols[0][0], cols[1][0]
            first = jnp.where(low58, one, pltpu.roll(two, 64, 1))
            second = jnp.where(low58, pltpu.roll(one, 64, 1), two)
            s0[p, 0:58, 0:128] = first
            s0[p, 0:58, 128:256] = second
            blocks = ((first, second), (cols[0][1], cols[1][1]), (cols[0][2], cols[1][2]))
            for t in range(3):
                for half in range(2):
                    narrow = blocks[t][half].astype(BF16)
                    xs[t * PER + p, 0:58, 128 * half : 128 * half + 128] = narrow
                    x0[t * PER + p, 0:58, 128 * half : 128 * half + 128] = narrow
        forcing = lax.dot_general(
            tc[...],
            gsc[...],
            (((1,), (1,)), ((), ())),
            precision=HIGHEST,
            preferred_element_type=F32,
        )
        for p in range(PER):
            turned = forcing if p == 0 else pltpu.roll(forcing, 128 - 16 * p, 1)
            hi = turned.astype(BF16)
            lf[p, :, 0:128] = hi
            lf[p, :, 128:256] = (turned - hi.astype(F32)).astype(BF16)
        both = lf[...].reshape(PER * 64, 256)
        for t in range(3):
            fs[t * PER : t * PER + PER] = _dot(both, spread[t]).reshape(PER, 64, 256)

        def substep(step, carry):
            h, v = hbd[...], vbd[...]
            for m in range(0, 3 * PER // 4, MERGE):
                x = xs[4 * m : 4 * (m + MERGE)].reshape(MERGE * 256, 256)
                all_mixed = _dot(x, h).astype(BF16)
                for q in range(m, m + MERGE):
                    mixed = all_mixed[256 * (q - m) : 256 * (q - m) + 256]
                    grown = jnp.tanh(_dot(v, mixed))
                    for i in range(4):
                        c = 4 * q + i
                        new = grown[64 * i : 64 * i + 64] + fs[c]
                        if c < PER:
                            one, two = s0[c, :, 0:128], s0[c, :, 128:256]
                            adjust = jnp.tanh(one * two) * avs[c] + one * bvs[c]
                            first, second = new[:, 0:128] + adjust, new[:, 128:256] - adjust
                            s0[c, :, 0:128] = first
                            s0[c, :, 128:256] = second
                            xs[c, :, 0:128] = first.astype(BF16)
                            xs[c, :, 128:256] = second.astype(BF16)
                        else:
                            xs[c] = new.astype(BF16)
            return carry

        lax.fori_loop(0, NSUB, substep, 0, unroll=UNROLL)

        mean = jnp.zeros((PER * 64, 128), F32)
        for t in range(3):
            diff = (xs[t * PER : t * PER + PER] - x0[t * PER : t * PER + PER]).reshape(PER * 64, 256)
            mean += _dot(diff, gather[t * 256 : t * 256 + 256, :])
        total = mean[0:64]
        for p in range(1, PER):
            total += pltpu.roll(mean[64 * p : 64 * p + 64], 16 * p, 1)
        tend = _dot(jnp.transpose(total), tg[...], precision=HIGHEST)
        for p in range(PER):
            for r in range(2):
                row = 16 * p + 8 * r
                tbuf[dests[p], r] = tend[row : row + 8]
                home = pl.ds(order[r, dests[p], 0], 1)
                updf[2 * p + r : 2 * p + r + 1, :] = tend[row : row + 1] + trt[r, home, :]
        usend[ch] = updf[...].astype(BF16)

        for p in range(PER):
            k = ch * PER + p
            one, two = s0[p, :, 0:128], s0[p, :, 128:256]
            left = jnp.where(low64, one, pltpu.roll(two, 64, 1)).astype(BF16)
            right = jnp.where(low64, pltpu.roll(one, 64, 1), two).astype(BF16)
            snd[k, 0, :, 0:128] = left[0:58]
            snd[k, 1, :, 0:128] = right[0:58]
            for t in (1, 2):
                for r in range(2):
                    snd[k, r, :, 128 * t : 128 * t + 128] = xs[
                        t * PER + p, 0:58, 128 * r : 128 * r + 128
                    ]

        @pl.when(ch == 0)
        def _():
            pl.semaphore_wait(barrier, NBLK - 1)
            for k in range(NBLK - 1):
                pack_copy(k).start()

        for k in range(NBLK - 1):
            tracer_copy(ch, k).start()
        own_tracer(ch).start()
        for j in range(PER - 1):
            state_copy(ch * PER + j, dests[j]).start()

        @pl.when(ch < CHUNKS - 1)
        def _():
            state_copy(ch * PER + PER - 1, dests[PER - 1]).start()

        return carry

    lax.fori_loop(0, CHUNKS, chunk, 0)

    own_state = pltpu.make_async_copy(snd.at[NBLK - 1], recv.at[me], self_sem)
    own_state.start()

    own_state.wait()
    own_pack.wait()
    for ch in range(CHUNKS):
        own_tracer(ch).wait()
    for k in range(NBLK - 1):
        pack_copy(k).wait()
        state_copy(k, peers[k]).wait()
        for ch in range(CHUNKS):
            tracer_copy(ch, k).wait()


def place(
    plan_s,
    recv,
    trec,
    prec,
    tbuf,
    shift,
    frac,
    state_out,
    tend_out,
    polar_out,
    rbuf,
    wide,
    obuf,
    tn,
    slots_v,
    slots_s,
    loop,
    cs,
    cf,
    in_sem,
    slot_sem,
    out_sem,
):
    me = lax.axis_index("lon")
    loads = [
        pltpu.make_async_copy(recv.at[pl.ds(8 * q, 8)], rbuf.at[pl.ds(8 * q, 8)], in_sem.at[q])
        for q in range(4)
    ]
    for load in loads:
        load.start()
    plans = prec[...]
    held = (plans // 32 == me) & (_iota((32, 8, 128), 2) < 32) & (_iota((32, 8, 128), 1) < 2)
    mine = jnp.where(held, plans % 32, 0)
    slots_v[...] = jnp.broadcast_to(jnp.max(mine, axis=2, keepdims=True), (32, 8, 128))
    to_smem = pltpu.make_async_copy(slots_v, slots_s, slot_sem)
    to_smem.start()

    for r in range(2):
        for i in range(32):
            tn[pl.ds(r * 6 * STEP + i, 6, stride=STEP), :] = tbuf[plan_s[r, i] // 32, r, 0:6, :]
        for f in range(6):
            at = (r * 6 + f) * STEP
            tend_out[r, f] = tn[at : at + 32, 0:72]

    target = _iota((64, 64), 0)
    for s in range(32):
        spots = jnp.broadcast_to(prec[s, 2:3, 0:64], (64, 64))
        rows = _dot(_onehot(spots == target), trec[s].reshape(64, 128))
        for r in range(2):
            loop[r, 32 * s : 32 * s + 32, :] = rows[32 * r : 32 * r + 32]

    cs[...] = jnp.zeros_like(cs)
    cf[...] = jnp.zeros_like(cf)
    cs[0:2, 0:72] = shift[...]
    cf[0:2, 0:72] = frac[...]
    for r in range(2):
        base = (me * 32 - 1 - cs[r : r + 1, :]) & 1023
        whole = loop[r]
        cut = jnp.concatenate([whole[512:1024], whole[0:32]], axis=0)
        now = jnp.where((base & 512) != 0, cut, whole[0:544])
        for size in (256, 128, 64, 32, 16, 8):
            rows = size + 32
            now = jnp.where((base & size) != 0, now[size : size + rows], now[0:rows])
        for size in (4, 2, 1):
            now = jnp.where((base & size) != 0, pltpu.roll(now, 40 - size, 0), now)
        weight = cf[r : r + 1, :]
        result = (1.0 - weight) * pltpu.roll(now, 39, 0) + weight * now
        polar_out[r] = result[0:32, 0:72]

    to_smem.wait()
    for q in range(4):
        loads[q].wait()

        def spot(s, carry):
            for r in range(2):
                column = rbuf[s, r].astype(F32)
                at = pl.ds(r * 58 * STEP + slots_s[s, r, 0], 58, stride=STEP)
                for t in range(3):
                    wide[t, at, :] = column[:, 128 * t : 128 * t + 128]
            return carry

        lax.fori_loop(8 * q, 8 * q + 8, spot, 0, unroll=2)

    outs = []
    for r in range(2):
        for part in range(2):

            def narrow(level, carry):
                for t in range(3):
                    obuf[r, level, :, 128 * t : 128 * t + 128] = wide[
                        t, pl.ds((r * 58 + level) * STEP, 32), :
                    ].astype(BF16)
                return carry

            lax.fori_loop(29 * part, 29 * part + 29, narrow, 0, unroll=True)
            piece = pl.ds(29 * part, 29)
            outs.append(
                pltpu.make_async_copy(
                    obuf.at[r, piece], state_out.at[r, piece], out_sem.at[2 * r + part]
                )
            )
            outs[-1].start()
    for out in outs:
        out.wait()


def per_device(
    crm_state,
    gcm_state,
    micro_flags,
    load_plan,
    h_mix,
    v_mix,
    to_crm,
    to_gcm,
    polar_tracer,
    courant_shift,
    courant_frac,
):
    smem = pl.BlockSpec(memory_space=pltpu.SMEM)
    vmem = pl.BlockSpec(memory_space=pltpu.VMEM)
    hbm = pl.BlockSpec(memory_space=pl.ANY)
    dma = pltpu.SemaphoreType.DMA
    recv, trec, prec, tbuf = pl.pallas_call(
        advance,
        out_shape=(
            jax.ShapeDtypeStruct((32, 2, 58, 384), BF16),
            jax.ShapeDtypeStruct((32, CHUNKS, 2 * PER, 128), BF16),
            jax.ShapeDtypeStruct((32, 8, 128), jnp.int32),
            jax.ShapeDtypeStruct((32, 2, 8, 128), F32),
        ),
        in_specs=[smem, vmem, hbm] + [vmem] * 6,
        out_specs=(hbm, hbm, hbm, vmem),
        scratch_shapes=[
            pltpu.VMEM((2, 58, 32, 384), BF16),
            pltpu.VMEM((3, 2 * 58 * STEP, 128), F32),
            pltpu.VMEM((3 * PER, 64, 256), BF16),
            pltpu.VMEM((3 * PER, 64, 256), BF16),
            pltpu.VMEM((PER, 64, 256), F32),
            pltpu.VMEM((3 * PER, 64, 256), F32),
            pltpu.VMEM((PER, 64, 256), BF16),
            pltpu.VMEM((2 * 6 * STEP, 128), F32),
            pltpu.VMEM((128, 128), F32),
            pltpu.VMEM((256, 256), BF16),
            pltpu.VMEM((256, 256), BF16),
            pltpu.VMEM((3, 256, 256), BF16),
            pltpu.VMEM((768, 128), BF16),
            pltpu.VMEM((64, 128), F32),
            pltpu.VMEM((64, 128), F32),
            pltpu.VMEM((2, 32, 128), F32),
            pltpu.VMEM((2 * PER, 128), F32),
            pltpu.VMEM((CHUNKS, 2 * PER, 128), BF16),
            pltpu.VMEM((32, 2, 58, 384), BF16),
            pltpu.VMEM((8, 128), jnp.int32),
            pltpu.VMEM((2, 32, 128), jnp.int32),
            pltpu.SMEM((2, 32, 128), jnp.int32),
            dma((2,)),
            dma,
            dma,
            dma((NBLK,)),
            dma((NBLK,)),
            dma((NBLK,)),
            dma((NBLK,)),
            dma((CHUNKS, NBLK)),
            dma((CHUNKS, NBLK)),
        ],
        compiler_params=pltpu.CompilerParams(collective_id=0, has_side_effects=True),
        name="advance",
    )(
        micro_flags,
        load_plan,
        jnp.transpose(crm_state, (0, 2, 1, 3)),
        jnp.transpose(gcm_state, (0, 2, 1, 3)),
        h_mix,
        v_mix,
        to_crm,
        to_gcm.T,
        jnp.transpose(polar_tracer, (0, 2, 1)),
    )
    new_state, tendency, polar_next = pl.pallas_call(
        place,
        out_shape=(
            jax.ShapeDtypeStruct((2, 58, 32, 384), BF16),
            jax.ShapeDtypeStruct((2, 6, 32, 72), F32),
            jax.ShapeDtypeStruct((2, 32, 72), F32),
        ),
        in_specs=[smem, hbm] + [vmem] * 5,
        out_specs=(hbm, vmem, vmem),
        scratch_shapes=[
            pltpu.VMEM((32, 2, 58, 384), BF16),
            pltpu.VMEM((3, 2 * 58 * STEP, 128), F32),
            pltpu.VMEM((2, 58, 32, 384), BF16),
            pltpu.VMEM((2 * 6 * STEP, 128), F32),
            pltpu.VMEM((32, 8, 128), jnp.int32),
            pltpu.SMEM((32, 8, 128), jnp.int32),
            pltpu.VMEM((2, 1024, 128), F32),
            pltpu.VMEM((8, 128), jnp.int32),
            pltpu.VMEM((8, 128), F32),
            dma((4,)),
            dma,
            dma((4,)),
        ],
        name="place",
    )(load_plan, recv, trec, prec, tbuf, courant_shift, courant_frac)
    return (
        jnp.transpose(new_state, (0, 2, 1, 3)),
        jnp.transpose(tendency, (0, 2, 1, 3)),
        jnp.transpose(polar_next, (0, 2, 1)),
    )


def solution(mesh):
    in_specs = (
        P("lat", "lon", None, None),
        P("lat", "lon", None, None),
        P("lat", "lon"),
        P("lat", "lon"),
        P(),
        P(),
        P(),
        P(),
        P("lat", None, "lon"),
        P("lat", None),
        P("lat", None),
    )
    out_specs = (P("lat", "lon", None, None), P("lat", "lon", None, None), P("lat", None, "lon"))
    return jax.shard_map(
        per_device, mesh=mesh, in_specs=in_specs, out_specs=out_specs, check_vma=False
    )
```

```python
import functools

import jax
import jax.numpy as jnp
from jax import lax
from jax.experimental import pallas as pl
from jax.experimental.pallas import tpu as pltpu
from jax.sharding import PartitionSpec as P

NSUB = 18
MESH = pl.DeviceIdType.MESH
F32 = jnp.float32
BF16 = jnp.bfloat16
HIGHEST = lax.Precision.HIGHEST

SIZES = (4, 4, 2)


def _hops(off):
    return sum(min(d, n - d) for d, n in zip(off, SIZES))


OFFSETS = sorted(
    ((a, b, c) for a in range(4) for b in range(4) for c in range(2)),
    key=lambda off: (-_hops(off), off),
)
OFFSETS = OFFSETS[0:8] + OFFSETS[16:24] + OFFSETS[8:16] + OFFSETS[24:32]
GUEST = 1
NBLK = len(OFFSETS)
CHUNKS = 4
PER = NBLK // CHUNKS
GROUPS = ((0, 8, 1, 9), (2, 3, 10, 11), (4, 5, 12, 13))
UNROLL = 18
MERGE = 3
STEP = 33


def _shifted(me, off):
    x, z, y = me // 8, (me // 2) % 4, me % 2
    return ((x + off[0]) % 4) * 8 + ((z + off[1]) % 4) * 2 + (y + off[2]) % 2


def _pick(index, values):
    out = jnp.int32(values[0])
    for i, value in enumerate(values[1:], 1):
        out = jnp.where(index == i, jnp.int32(value), out)
    return out


def _iota(shape, axis):
    return lax.broadcasted_iota(jnp.int32, shape, axis)


def _dot(a, b, **kw):
    return jnp.dot(a, b, preferred_element_type=F32, **kw)


def _onehot(mask):
    return jnp.where(mask, jnp.float32(1), jnp.float32(0)).astype(BF16)


def _lane_map(quarter, lanes):
    out = jnp.full(quarter.shape, lanes[0], jnp.int32)
    for i, lane in enumerate(lanes[1:], 1):
        out = jnp.where(quarter == i, lane, out)
    return out


def advance(
    flags,
    plan_v,
    crm,
    gcm,
    h_ref,
    v_ref,
    to_crm,
    to_gcm,
    tracer,
    recv,
    trec,
    prec,
    tbuf,
    crm_v,
    cn,
    xs,
    x0,
    s0,
    fs,
    lf,
    gn,
    gsc,
    hbd,
    vbd,
    spread,
    gather,
    tc,
    tg,
    trt,
    updf,
    usend,
    snd,
    raw,
    gsnd,
    graw,
    tout,
    tsnd,
    tback,
    pack,
    order_v,
    order,
    in_sem,
    order_sem,
    self_sem,
    ssem,
    rsem,
    pssem,
    prsem,
    tssem,
    trsem,
    gssem,
    grsem,
    bssem,
    brsem,
):
    me = lax.axis_index("lon")
    loads = [pltpu.make_async_copy(crm.at[r], crm_v.at[r], in_sem.at[r]) for r in range(2)]
    for load in loads:
        load.start()

    peers = [_shifted(me, off) for off in OFFSETS]
    barrier = pltpu.get_barrier_semaphore()
    for k in range(NBLK - 1):
        pl.semaphore_signal(barrier, inc=1, device_id={"lon": peers[k]}, device_id_type=MESH)

    for r in range(2):
        owners = jnp.broadcast_to(plan_v[r : r + 1, :] // 32, (32, 32))
        at = jnp.where(owners == _iota((32, 32), 0), _iota((32, 32), 1), 0)
        order_v[r] = jnp.broadcast_to(jnp.max(at, axis=1, keepdims=True), (32, 128))
    lane = _iota((1, 128), 1)
    bound = jnp.full((1, 128), 64, jnp.int32)
    for k in range(NBLK):
        bound = jnp.where(lane // 2 == k, peers[k], bound)
    value = jnp.where(_iota((32, 128), 1) % 2 == 0, order_v[0], order_v[1] + 32)
    spot = jnp.where(bound == _iota((32, 128), 0), value, 0)
    pack[...] = jnp.zeros_like(pack)
    pack[0:2, 0:32] = plan_v[...]
    pack[2:3, :] = jnp.max(spot, axis=0, keepdims=True)
    to_smem = pltpu.make_async_copy(order_v, order, order_sem)
    to_smem.start()

    tile_h = _onehot(_iota((64, 256), 1) % 64 == _iota((64, 256), 0))
    tile_ht = _onehot(_iota((256, 64), 0) % 64 == _iota((256, 64), 1))
    tile_v = _onehot(_iota((58, 256), 1) % 64 == _iota((58, 256), 0))
    tile_vt = _onehot(_iota((256, 58), 0) % 64 == _iota((256, 58), 1))
    diag = _iota((256, 256), 0) // 64 == _iota((256, 256), 1) // 64
    h_rep = _dot(_dot(tile_ht, h_ref[...]).astype(BF16), tile_h)
    v_rep = _dot(_dot(tile_vt, v_ref[...]).astype(BF16), tile_v)
    hbd[...] = jnp.where(diag, h_rep, 0.0).astype(BF16)
    vbd[...] = jnp.where(diag, v_rep, 0.0).astype(BF16)
    for t, lanes in enumerate(GROUPS):
        spread[t] = _onehot(_iota((256, 256), 0) % 128 == _lane_map(_iota((256, 256), 1) // 64, lanes))
        hit = _iota((256, 128), 1) == _lane_map(_iota((256, 128), 0) // 64, lanes)
        gather[t * 256 : t * 256 + 256, :] = jnp.where(hit, jnp.float32(1.0 / 64), 0.0).astype(BF16)
    tc[...] = jnp.zeros_like(tc)
    tc[0:58, 0:72] = 0.5 * to_crm[...]
    tg[...] = jnp.zeros_like(tg)
    tg[0:58, 0:72] = to_gcm[...]
    gsc[...] = jnp.zeros_like(gsc)
    gn[...] = jnp.zeros_like(gn)
    xs[...] = jnp.zeros_like(xs)
    x0[...] = jnp.zeros_like(x0)
    s0[...] = jnp.zeros_like(s0)
    trt[...] = jnp.zeros_like(trt)
    for r in range(2):
        trt[r, :, 0:72] = tracer[r]
        for f in range(6):
            gn[(r * 6 + f) * STEP : (r * 6 + f) * STEP + 32, 0:72] = gcm[r, f].astype(F32)

    for r in range(2):
        loads[r].wait()

        def widen(level, carry):
            block = crm_v[r, level].astype(F32)
            for t in range(3):
                cn[t, pl.ds((r * 58 + level) * STEP, 32), :] = block[:, 128 * t : 128 * t + 128]
            return carry

        lax.fori_loop(0, 58, widen, 0, unroll=2)
    to_smem.wait()
    low58 = _iota((58, 128), 1) < 64
    low64 = _iota((64, 128), 1) < 64
    low1 = _iota((1, 128), 1) < 64

    def pack_copy(k):
        return pltpu.make_async_remote_copy(
            src_ref=pack,
            dst_ref=prec.at[me],
            send_sem=pssem.at[k],
            recv_sem=prsem.at[k],
            device_id={"lon": peers[k]},
            device_id_type=MESH,
        )

    own_pack = pltpu.make_async_copy(pack, prec.at[me], pssem.at[NBLK - 1])
    own_pack.start()

    def tracer_copy(ch, k):
        return pltpu.make_async_remote_copy(
            src_ref=usend.at[ch],
            dst_ref=trec.at[me, ch],
            send_sem=tssem.at[ch, k],
            recv_sem=trsem.at[ch, k],
            device_id={"lon": peers[k]},
            device_id_type=MESH,
        )

    def own_tracer(ch):
        return pltpu.make_async_copy(usend.at[ch], trec.at[me, ch], tssem.at[ch, NBLK - 1])

    def state_copy(k, dest):
        return pltpu.make_async_remote_copy(
            src_ref=snd.at[k],
            dst_ref=recv.at[me],
            send_sem=ssem.at[k],
            recv_sem=rsem.at[k],
            device_id={"lon": dest},
            device_id_type=MESH,
        )

    guests = [GUEST * PER + p for p in range(PER)]
    homes = [_shifted(me, [(n - d) % n for d, n in zip(OFFSETS[k], SIZES)]) for k in guests]

    def raw_copy(p):
        return pltpu.make_async_remote_copy(
            src_ref=snd.at[guests[p]],
            dst_ref=raw.at[p],
            send_sem=ssem.at[guests[p]],
            recv_sem=rsem.at[guests[p]],
            device_id={"lon": peers[guests[p]]},
            device_id_type=MESH,
        )

    def gcm_copy(p):
        return pltpu.make_async_remote_copy(
            src_ref=gsnd.at[p],
            dst_ref=graw.at[p],
            send_sem=gssem.at[p],
            recv_sem=grsem.at[p],
            device_id={"lon": peers[guests[p]]},
            device_id_type=MESH,
        )

    def back_copy(p):
        return pltpu.make_async_remote_copy(
            src_ref=tsnd.at[p],
            dst_ref=tback.at[p],
            send_sem=bssem.at[p],
            recv_sem=brsem.at[p],
            device_id={"lon": homes[p]},
            device_id_type=MESH,
        )

    def guest_copy(p):
        return pltpu.make_async_copy(snd.at[guests[p]], recv.at[homes[p]], self_sem.at[p])

    def fetch(r, i):
        column = [cn[t, pl.ds(r * 58 * STEP + i, 58, stride=STEP), :] for t in range(3)]
        flag = jnp.where(flags[r, i] == 1, jnp.float32(1), jnp.float32(0))
        return column, gn[pl.ds(r * 6 * STEP + i, 6, stride=STEP), :], jnp.full((1, 128), flag)

    gsnd[...] = jnp.zeros_like(gsnd)
    for p in range(PER):
        for r in range(2):
            column, model, flag = fetch(r, order[r, peers[guests[p]], 0])
            for t in range(3):
                snd[guests[p], r, :, 128 * t : 128 * t + 128] = column[t].astype(BF16)
            gsnd[p, 8 * r : 8 * r + 6, :] = model
            gsnd[p, 8 * r + 6 : 8 * r + 7, :] = flag
    pl.semaphore_wait(barrier, NBLK - 1)
    for p in range(PER):
        raw_copy(p).start()
        gcm_copy(p).start()
    for k in range(NBLK - 1):
        pack_copy(k).start()

    def enter(p, one, two):
        first = jnp.where(low58, one[0], pltpu.roll(two[0], 64, 1))
        second = jnp.where(low58, pltpu.roll(one[0], 64, 1), two[0])
        s0[p, 0:58, 0:128] = first
        s0[p, 0:58, 128:256] = second
        blocks = ((first, second), (one[1], two[1]), (one[2], two[2]))
        for t in range(3):
            for half in range(2):
                narrow = blocks[t][half].astype(BF16)
                xs[t * PER + p, 0:58, 128 * half : 128 * half + 128] = narrow
                x0[t * PER + p, 0:58, 128 * half : 128 * half + 128] = narrow

    def tell(ch, places, rows):
        for p in range(PER):
            for r in range(2):
                home = pl.ds(order[r, places[p], 0], 1)
                tbuf[places[p], r] = rows[p, r]
                updf[2 * p + r : 2 * p + r + 1, :] = rows[p, r, 0:1, :] + trt[r, home, :]
        usend[ch] = updf[...].astype(BF16)
        for k in range(NBLK - 1):
            tracer_copy(ch, k).start()
        own_tracer(ch).start()

    def chunk(ch, carry):
        dests = []
        for j in range(PER):
            offs = [OFFSETS[c * PER + j] for c in range(CHUNKS)]
            off = [_pick(ch, [o[i] for o in offs]) for i in range(3)]
            dests.append(_shifted(me, off))

        @pl.when(ch != GUEST)
        def _():
            for p in range(PER):
                pair = []
                for r in range(2):
                    column, model, flag = fetch(r, order[r, dests[p], 0])
                    row = 16 * p + 8 * r
                    gsc[row : row + 6, :] = model
                    gsc[row + 6 : row + 7, :] = flag
                    pair.append(column)
                enter(p, *pair)

        @pl.when(ch == GUEST)
        def _():
            for p in range(PER):
                raw_copy(p).wait()
                gcm_copy(p).wait()
            for p in range(PER):
                pair = []
                for r in range(2):
                    column = raw[p, r].astype(F32)
                    pair.append([column[:, 128 * t : 128 * t + 128] for t in range(3)])
                gsc[16 * p : 16 * p + 16, :] = graw[p]
                enter(p, *pair)

        avs, bvs = [], []
        for p in range(PER):
            row = 16 * p + 6
            flag = jnp.where(low1, gsc[row : row + 1, :], gsc[row + 8 : row + 9, :])
            avs.append(0.5 * flag)
            bvs.append(0.25 * flag - 0.25)
        forcing = lax.dot_general(
            tc[...],
            gsc[...],
            (((1,), (1,)), ((), ())),
            precision=HIGHEST,
            preferred_element_type=F32,
        )
        for p in range(PER):
            turned = forcing if p == 0 else pltpu.roll(forcing, 128 - 16 * p, 1)
            hi = turned.astype(BF16)
            lf[p, :, 0:128] = hi
            lf[p, :, 128:256] = (turned - hi.astype(F32)).astype(BF16)
        both = lf[...].reshape(PER * 64, 256)
        for t in range(3):
            fs[t * PER : t * PER + PER] = _dot(both, spread[t]).reshape(PER, 64, 256)

        def substep(step, carry):
            h, v = hbd[...], vbd[...]
            for m in range(0, 3 * PER // 4, MERGE):
                x = xs[4 * m : 4 * (m + MERGE)].reshape(MERGE * 256, 256)
                all_mixed = _dot(x, h).astype(BF16)
                for q in range(m, m + MERGE):
                    mixed = all_mixed[256 * (q - m) : 256 * (q - m) + 256]
                    grown = jnp.tanh(_dot(v, mixed))
                    for i in range(4):
                        c = 4 * q + i
                        new = grown[64 * i : 64 * i + 64] + fs[c]
                        if c < PER:
                            one, two = s0[c, :, 0:128], s0[c, :, 128:256]
                            adjust = jnp.tanh(one * two) * avs[c] + one * bvs[c]
                            first, second = new[:, 0:128] + adjust, new[:, 128:256] - adjust
                            s0[c, :, 0:128] = first
                            s0[c, :, 128:256] = second
                            xs[c, :, 0:128] = first.astype(BF16)
                            xs[c, :, 128:256] = second.astype(BF16)
                        else:
                            xs[c] = new.astype(BF16)
            return carry

        lax.fori_loop(0, NSUB, substep, 0, unroll=UNROLL)

        mean = jnp.zeros((PER * 64, 128), F32)
        for t in range(3):
            diff = (xs[t * PER : t * PER + PER] - x0[t * PER : t * PER + PER]).reshape(PER * 64, 256)
            mean += _dot(diff, gather[t * 256 : t * 256 + 256, :])
        total = mean[0:64]
        for p in range(1, PER):
            total += pltpu.roll(mean[64 * p : 64 * p + 64], 16 * p, 1)
        tend = _dot(jnp.transpose(total), tg[...], precision=HIGHEST)
        for p in range(PER):
            for r in range(2):
                row = 16 * p + 8 * r
                tout[p, r] = tend[row : row + 8]

        for p in range(PER):
            k = ch * PER + p
            one, two = s0[p, :, 0:128], s0[p, :, 128:256]
            left = jnp.where(low64, one, pltpu.roll(two, 64, 1)).astype(BF16)
            right = jnp.where(low64, pltpu.roll(one, 64, 1), two).astype(BF16)
            snd[k, 0, :, 0:128] = left[0:58]
            snd[k, 1, :, 0:128] = right[0:58]
            for t in (1, 2):
                for r in range(2):
                    snd[k, r, :, 128 * t : 128 * t + 128] = xs[
                        t * PER + p, 0:58, 128 * r : 128 * r + 128
                    ]

        @pl.when(ch != GUEST)
        def _():
            tell(ch, dests, tout)
            for j in range(PER - 1):
                state_copy(ch * PER + j, dests[j]).start()

        @pl.when((ch != GUEST) & (ch < CHUNKS - 1))
        def _():
            state_copy(ch * PER + PER - 1, dests[PER - 1]).start()

        @pl.when(ch == GUEST)
        def _():
            tsnd[...] = tout[...]
            for p in range(PER):
                back_copy(p).start()
                guest_copy(p).start()

        @pl.when(ch == GUEST + 1)
        def _():
            for p in range(PER):
                back_copy(p).wait()
            tell(GUEST, [peers[k] for k in guests], tback)

        return carry

    lax.fori_loop(0, CHUNKS, chunk, 0)

    own_state = pltpu.make_async_copy(snd.at[NBLK - 1], recv.at[me], self_sem.at[PER])
    own_state.start()

    own_state.wait()
    own_pack.wait()
    for ch in range(CHUNKS):
        own_tracer(ch).wait()
    for p in range(PER):
        guest_copy(p).wait()
    for k in range(NBLK - 1):
        pack_copy(k).wait()
        if k not in guests:
            state_copy(k, peers[k]).wait()
        for ch in range(CHUNKS):
            tracer_copy(ch, k).wait()


def place(
    plan_s,
    recv,
    trec,
    prec,
    tbuf,
    shift,
    frac,
    state_out,
    tend_out,
    polar_out,
    rbuf,
    wide,
    obuf,
    tn,
    slots_v,
    slots_s,
    loop,
    cs,
    cf,
    in_sem,
    slot_sem,
    out_sem,
):
    me = lax.axis_index("lon")
    loads = [
        pltpu.make_async_copy(recv.at[pl.ds(8 * q, 8)], rbuf.at[pl.ds(8 * q, 8)], in_sem.at[q])
        for q in range(4)
    ]
    for load in loads:
        load.start()
    plans = prec[...]
    held = (plans // 32 == me) & (_iota((32, 8, 128), 2) < 32) & (_iota((32, 8, 128), 1) < 2)
    mine = jnp.where(held, plans % 32, 0)
    slots_v[...] = jnp.broadcast_to(jnp.max(mine, axis=2, keepdims=True), (32, 8, 128))
    to_smem = pltpu.make_async_copy(slots_v, slots_s, slot_sem)
    to_smem.start()

    for r in range(2):
        for i in range(32):
            tn[pl.ds(r * 6 * STEP + i, 6, stride=STEP), :] = tbuf[plan_s[r, i] // 32, r, 0:6, :]
        for f in range(6):
            at = (r * 6 + f) * STEP
            tend_out[r, f] = tn[at : at + 32, 0:72]

    target = _iota((64, 64), 0)
    for s in range(32):
        spots = jnp.broadcast_to(prec[s, 2:3, 0:64], (64, 64))
        rows = _dot(_onehot(spots == target), trec[s].reshape(64, 128))
        for r in range(2):
            loop[r, 32 * s : 32 * s + 32, :] = rows[32 * r : 32 * r + 32]

    cs[...] = jnp.zeros_like(cs)
    cf[...] = jnp.zeros_like(cf)
    cs[0:2, 0:72] = shift[...]
    cf[0:2, 0:72] = frac[...]
    for r in range(2):
        base = (me * 32 - 1 - cs[r : r + 1, :]) & 1023
        whole = loop[r]
        cut = jnp.concatenate([whole[512:1024], whole[0:32]], axis=0)
        now = jnp.where((base & 512) != 0, cut, whole[0:544])
        for size in (256, 128, 64, 32, 16, 8):
            rows = size + 32
            now = jnp.where((base & size) != 0, now[size : size + rows], now[0:rows])
        for size in (4, 2, 1):
            now = jnp.where((base & size) != 0, pltpu.roll(now, 40 - size, 0), now)
        weight = cf[r : r + 1, :]
        result = (1.0 - weight) * pltpu.roll(now, 39, 0) + weight * now
        polar_out[r] = result[0:32, 0:72]

    to_smem.wait()
    for q in range(4):
        loads[q].wait()

        def spot(s, carry):
            for r in range(2):
                column = rbuf[s, r].astype(F32)
                at = pl.ds(r * 58 * STEP + slots_s[s, r, 0], 58, stride=STEP)
                for t in range(3):
                    wide[t, at, :] = column[:, 128 * t : 128 * t + 128]
            return carry

        lax.fori_loop(8 * q, 8 * q + 8, spot, 0, unroll=2)

    outs = []
    for r in range(2):
        for part in range(2):

            def narrow(level, carry):
                for t in range(3):
                    obuf[r, level, :, 128 * t : 128 * t + 128] = wide[
                        t, pl.ds((r * 58 + level) * STEP, 32), :
                    ].astype(BF16)
                return carry

            lax.fori_loop(29 * part, 29 * part + 29, narrow, 0, unroll=True)
            piece = pl.ds(29 * part, 29)
            outs.append(
                pltpu.make_async_copy(
                    obuf.at[r, piece], state_out.at[r, piece], out_sem.at[2 * r + part]
                )
            )
            outs[-1].start()
    for out in outs:
        out.wait()


def per_device(
    crm_state,
    gcm_state,
    micro_flags,
    load_plan,
    h_mix,
    v_mix,
    to_crm,
    to_gcm,
    polar_tracer,
    courant_shift,
    courant_frac,
):
    smem = pl.BlockSpec(memory_space=pltpu.SMEM)
    vmem = pl.BlockSpec(memory_space=pltpu.VMEM)
    hbm = pl.BlockSpec(memory_space=pl.ANY)
    dma = pltpu.SemaphoreType.DMA
    recv, trec, prec, tbuf = pl.pallas_call(
        advance,
        out_shape=(
            jax.ShapeDtypeStruct((32, 2, 58, 384), BF16),
            jax.ShapeDtypeStruct((32, CHUNKS, 2 * PER, 128), BF16),
            jax.ShapeDtypeStruct((32, 8, 128), jnp.int32),
            jax.ShapeDtypeStruct((32, 2, 8, 128), F32),
        ),
        in_specs=[smem, vmem, hbm] + [vmem] * 6,
        out_specs=(hbm, hbm, hbm, vmem),
        scratch_shapes=[
            pltpu.VMEM((2, 58, 32, 384), BF16),
            pltpu.VMEM((3, 2 * 58 * STEP, 128), F32),
            pltpu.VMEM((3 * PER, 64, 256), BF16),
            pltpu.VMEM((3 * PER, 64, 256), BF16),
            pltpu.VMEM((PER, 64, 256), F32),
            pltpu.VMEM((3 * PER, 64, 256), F32),
            pltpu.VMEM((PER, 64, 256), BF16),
            pltpu.VMEM((2 * 6 * STEP, 128), F32),
            pltpu.VMEM((128, 128), F32),
            pltpu.VMEM((256, 256), BF16),
            pltpu.VMEM((256, 256), BF16),
            pltpu.VMEM((3, 256, 256), BF16),
            pltpu.VMEM((768, 128), BF16),
            pltpu.VMEM((64, 128), F32),
            pltpu.VMEM((64, 128), F32),
            pltpu.VMEM((2, 32, 128), F32),
            pltpu.VMEM((2 * PER, 128), F32),
            pltpu.VMEM((CHUNKS, 2 * PER, 128), BF16),
            pltpu.VMEM((32, 2, 58, 384), BF16),
            pltpu.VMEM((PER, 2, 58, 384), BF16),
            pltpu.VMEM((PER, 16, 128), F32),
            pltpu.VMEM((PER, 16, 128), F32),
            pltpu.VMEM((PER, 2, 8, 128), F32),
            pltpu.VMEM((PER, 2, 8, 128), F32),
            pltpu.VMEM((PER, 2, 8, 128), F32),
            pltpu.VMEM((8, 128), jnp.int32),
            pltpu.VMEM((2, 32, 128), jnp.int32),
            pltpu.SMEM((2, 32, 128), jnp.int32),
            dma((2,)),
            dma,
            dma((PER + 1,)),
            dma((NBLK,)),
            dma((NBLK,)),
            dma((NBLK,)),
            dma((NBLK,)),
            dma((CHUNKS, NBLK)),
            dma((CHUNKS, NBLK)),
            dma((PER,)),
            dma((PER,)),
            dma((PER,)),
            dma((PER,)),
        ],
        compiler_params=pltpu.CompilerParams(collective_id=0, has_side_effects=True),
        name="advance",
    )(
        micro_flags,
        load_plan,
        jnp.transpose(crm_state, (0, 2, 1, 3)),
        jnp.transpose(gcm_state, (0, 2, 1, 3)),
        h_mix,
        v_mix,
        to_crm,
        to_gcm.T,
        jnp.transpose(polar_tracer, (0, 2, 1)),
    )
    new_state, tendency, polar_next = pl.pallas_call(
        place,
        out_shape=(
            jax.ShapeDtypeStruct((2, 58, 32, 384), BF16),
            jax.ShapeDtypeStruct((2, 6, 32, 72), F32),
            jax.ShapeDtypeStruct((2, 32, 72), F32),
        ),
        in_specs=[smem, hbm] + [vmem] * 5,
        out_specs=(hbm, vmem, vmem),
        scratch_shapes=[
            pltpu.VMEM((32, 2, 58, 384), BF16),
            pltpu.VMEM((3, 2 * 58 * STEP, 128), F32),
            pltpu.VMEM((2, 58, 32, 384), BF16),
            pltpu.VMEM((2 * 6 * STEP, 128), F32),
            pltpu.VMEM((32, 8, 128), jnp.int32),
            pltpu.SMEM((32, 8, 128), jnp.int32),
            pltpu.VMEM((2, 1024, 128), F32),
            pltpu.VMEM((8, 128), jnp.int32),
            pltpu.VMEM((8, 128), F32),
            dma((4,)),
            dma,
            dma((4,)),
        ],
        name="place",
    )(load_plan, recv, trec, prec, tbuf, courant_shift, courant_frac)
    return (
        jnp.transpose(new_state, (0, 2, 1, 3)),
        jnp.transpose(tendency, (0, 2, 1, 3)),
        jnp.transpose(polar_next, (0, 2, 1)),
    )


def solution(mesh):
    in_specs = (
        P("lat", "lon", None, None),
        P("lat", "lon", None, None),
        P("lat", "lon"),
        P("lat", "lon"),
        P(),
        P(),
        P(),
        P(),
        P("lat", None, "lon"),
        P("lat", None),
        P("lat", None),
    )
    out_specs = (P("lat", "lon", None, None), P("lat", "lon", None, None), P("lat", None, "lon"))
    return jax.shard_map(
        per_device, mesh=mesh, in_specs=in_specs, out_specs=out_specs, check_vma=False
    )
```

```python
import functools

import jax
import jax.numpy as jnp
from jax import lax
from jax.experimental import pallas as pl
from jax.experimental.pallas import tpu as pltpu
from jax.sharding import PartitionSpec as P

NSUB = 18
MESH = pl.DeviceIdType.MESH
F32 = jnp.float32
BF16 = jnp.bfloat16
HIGHEST = lax.Precision.HIGHEST

SIZES = (4, 4, 2)


def _hops(off):
    return sum(min(d, n - d) for d, n in zip(off, SIZES))


OFFSETS = sorted(
    ((a, b, c) for a in range(4) for b in range(4) for c in range(2)),
    key=lambda off: (-_hops(off), off),
)
NBLK = len(OFFSETS)
CHUNKS = 4
PER = NBLK // CHUNKS
GROUPS = ((0, 8, 1, 9), (2, 3, 10, 11), (4, 5, 12, 13))
UNROLL = 18
MERGE = 3
STEP = 33


def _shifted(me, off):
    x, z, y = me // 8, (me // 2) % 4, me % 2
    return ((x + off[0]) % 4) * 8 + ((z + off[1]) % 4) * 2 + (y + off[2]) % 2


def _pick(index, values):
    out = jnp.int32(values[0])
    for i, value in enumerate(values[1:], 1):
        out = jnp.where(index == i, jnp.int32(value), out)
    return out


def _iota(shape, axis):
    return lax.broadcasted_iota(jnp.int32, shape, axis)


def _dot(a, b, **kw):
    return jnp.dot(a, b, preferred_element_type=F32, **kw)


def _onehot(mask):
    return jnp.where(mask, jnp.float32(1), jnp.float32(0)).astype(BF16)


def _part(r, t):
    return slice(58 * (3 * r + t), 58 * (3 * r + t) + 58)


def _lane_map(quarter, lanes):
    out = jnp.full(quarter.shape, lanes[0], jnp.int32)
    for i, lane in enumerate(lanes[1:], 1):
        out = jnp.where(quarter == i, lane, out)
    return out


def advance(
    flags,
    plan_v,
    crm,
    gcm,
    h_ref,
    v_ref,
    to_crm,
    to_gcm,
    tracer,
    recv,
    trec,
    prec,
    tend_out,
    tbuf,
    crm_v,
    cn,
    xs,
    x0,
    s0,
    fs,
    lf,
    gn,
    gsc,
    hbd,
    vbd,
    spread,
    gather,
    tc,
    tg,
    trt,
    updf,
    usend,
    snd,
    pack,
    order_v,
    order,
    in_sem,
    order_sem,
    self_sem,
    tend_sem,
    ssem,
    rsem,
    pssem,
    prsem,
    tssem,
    trsem,
):
    me = lax.axis_index("lon")
    loads = [pltpu.make_async_copy(crm.at[r], crm_v.at[r], in_sem.at[r]) for r in range(2)]
    for load in loads:
        load.start()

    peers = [_shifted(me, off) for off in OFFSETS]
    barrier = pltpu.get_barrier_semaphore()
    for k in range(NBLK - 1):
        pl.semaphore_signal(barrier, inc=1, device_id={"lon": peers[k]}, device_id_type=MESH)

    for r in range(2):
        owners = jnp.broadcast_to(plan_v[r : r + 1, :] // 32, (32, 32))
        at = jnp.where(owners == _iota((32, 32), 0), _iota((32, 32), 1), 0)
        order_v[r] = jnp.broadcast_to(jnp.max(at, axis=1, keepdims=True), (32, 128))
    lane = _iota((1, 128), 1)
    bound = jnp.full((1, 128), 64, jnp.int32)
    for k in range(NBLK):
        bound = jnp.where(lane // 2 == k, peers[k], bound)
    value = jnp.where(_iota((32, 128), 1) % 2 == 0, order_v[0], order_v[1] + 32)
    spot = jnp.where(bound == _iota((32, 128), 0), value, 0)
    pack[...] = jnp.zeros_like(pack)
    pack[0:2, 0:32] = plan_v[...]
    pack[2:3, :] = jnp.max(spot, axis=0, keepdims=True)
    to_smem = pltpu.make_async_copy(order_v, order, order_sem)
    to_smem.start()

    tile_h = _onehot(_iota((64, 256), 1) % 64 == _iota((64, 256), 0))
    tile_ht = _onehot(_iota((256, 64), 0) % 64 == _iota((256, 64), 1))
    tile_v = _onehot(_iota((58, 256), 1) % 64 == _iota((58, 256), 0))
    tile_vt = _onehot(_iota((256, 58), 0) % 64 == _iota((256, 58), 1))
    diag = _iota((256, 256), 0) // 64 == _iota((256, 256), 1) // 64
    h_rep = _dot(_dot(tile_ht, h_ref[...]).astype(BF16), tile_h)
    v_rep = _dot(_dot(tile_vt, v_ref[...]).astype(BF16), tile_v)
    hbd[...] = jnp.where(diag, h_rep, 0.0).astype(BF16)
    vbd[...] = jnp.where(diag, v_rep, 0.0).astype(BF16)
    for t, lanes in enumerate(GROUPS):
        spread[t] = _onehot(_iota((256, 256), 0) % 128 == _lane_map(_iota((256, 256), 1) // 64, lanes))
        hit = _iota((256, 128), 1) == _lane_map(_iota((256, 128), 0) // 64, lanes)
        gather[t * 256 : t * 256 + 256, :] = jnp.where(hit, jnp.float32(1.0 / 64), 0.0).astype(BF16)
    tc[...] = jnp.zeros_like(tc)
    tc[0:58, 0:72] = 0.5 * to_crm[...]
    tg[...] = jnp.zeros_like(tg)
    tg[0:58, 0:72] = to_gcm[...]
    gsc[...] = jnp.zeros_like(gsc)
    gn[...] = jnp.zeros_like(gn)
    xs[...] = jnp.zeros_like(xs)
    x0[...] = jnp.zeros_like(x0)
    s0[...] = jnp.zeros_like(s0)
    trt[...] = jnp.zeros_like(trt)
    for r in range(2):
        trt[r, :, 0:72] = tracer[r]
        for f in range(6):
            gn[(r * 6 + f) * STEP : (r * 6 + f) * STEP + 32, 0:72] = gcm[r, f].astype(F32)

    for r in range(2):
        loads[r].wait()

        def widen(level, carry):
            block = crm_v[r, level].astype(F32)
            for t in range(3):
                cn[t, pl.ds((r * 58 + level) * STEP, 32), :] = block[:, 128 * t : 128 * t + 128]
            return carry

        lax.fori_loop(0, 58, widen, 0, unroll=2)
    to_smem.wait()

    def pack_copy(k):
        return pltpu.make_async_remote_copy(
            src_ref=pack,
            dst_ref=prec.at[me],
            send_sem=pssem.at[k],
            recv_sem=prsem.at[k],
            device_id={"lon": peers[k]},
            device_id_type=MESH,
        )

    own_pack = pltpu.make_async_copy(pack, prec.at[me], pssem.at[NBLK - 1])
    own_pack.start()

    def tracer_copy(ch, k):
        return pltpu.make_async_remote_copy(
            src_ref=usend.at[ch],
            dst_ref=trec.at[me, ch],
            send_sem=tssem.at[ch, k],
            recv_sem=trsem.at[ch, k],
            device_id={"lon": peers[k]},
            device_id_type=MESH,
        )

    def own_tracer(ch):
        return pltpu.make_async_copy(usend.at[ch], trec.at[me, ch], tssem.at[ch, NBLK - 1])

    low58 = _iota((58, 128), 1) < 64
    low64 = _iota((64, 128), 1) < 64
    low1 = _iota((1, 128), 1) < 64

    def state_copy(k, dest):
        return pltpu.make_async_remote_copy(
            src_ref=snd.at[k],
            dst_ref=recv.at[me],
            send_sem=ssem.at[k],
            recv_sem=rsem.at[k],
            device_id={"lon": dest},
            device_id_type=MESH,
        )

    def chunk(ch, carry):
        dests = []
        for j in range(PER):
            offs = [OFFSETS[c * PER + j] for c in range(CHUNKS)]
            off = [_pick(ch, [o[i] for o in offs]) for i in range(3)]
            dests.append(_shifted(me, off))
        avs, bvs = [], []
        for p in range(PER):
            cols, a, b = [], [], []
            for r in range(2):
                i = order[r, dests[p], 0]
                cols.append([cn[t, pl.ds(r * 58 * STEP + i, 58, stride=STEP), :] for t in range(3)])
                row = 16 * p + 8 * r
                gsc[row : row + 6, :] = gn[pl.ds(r * 6 * STEP + i, 6, stride=STEP), :]
                flag = flags[r, i]
                a.append(jnp.where(flag == 1, jnp.float32(0.5), jnp.float32(0)))
                b.append(jnp.where(flag == 1, jnp.float32(0), jnp.float32(-0.25)))
            avs.append(jnp.where(low1, a[0], a[1]))
            bvs.append(jnp.where(low1, b[0], b[1]))
            one, two = cols[0][0], cols[1][0]
            first = jnp.where(low58, one, pltpu.roll(two, 64, 1))
            second = jnp.where(low58, pltpu.roll(one, 64, 1), two)
            s0[p, 0:58, 0:128] = first
            s0[p, 0:58, 128:256] = second
            blocks = ((first, second), (cols[0][1], cols[1][1]), (cols[0][2], cols[1][2]))
            for t in range(3):
                for half in range(2):
                    narrow = blocks[t][half].astype(BF16)
                    xs[t * PER + p, 0:58, 128 * half : 128 * half + 128] = narrow
                    x0[t * PER + p, 0:58, 128 * half : 128 * half + 128] = narrow
        forcing = lax.dot_general(
            tc[...],
            gsc[...],
            (((1,), (1,)), ((), ())),
            precision=HIGHEST,
            preferred_element_type=F32,
        )
        for p in range(PER):
            turned = forcing if p == 0 else pltpu.roll(forcing, 128 - 16 * p, 1)
            hi = turned.astype(BF16)
            lf[p, :, 0:128] = hi
            lf[p, :, 128:256] = (turned - hi.astype(F32)).astype(BF16)
        both = lf[...].reshape(PER * 64, 256)
        for t in range(3):
            fs[t * PER : t * PER + PER] = _dot(both, spread[t]).reshape(PER, 64, 256)

        def substep(step, carry):
            h, v = hbd[...], vbd[...]
            for m in range(0, 3 * PER // 4, MERGE):
                x = xs[4 * m : 4 * (m + MERGE)].reshape(MERGE * 256, 256)
                all_mixed = _dot(x, h).astype(BF16)
                for q in range(m, m + MERGE):
                    mixed = all_mixed[256 * (q - m) : 256 * (q - m) + 256]
                    grown = jnp.tanh(_dot(v, mixed))
                    for i in range(4):
                        c = 4 * q + i
                        new = grown[64 * i : 64 * i + 64] + fs[c]
                        if c < PER:
                            one, two = s0[c, :, 0:128], s0[c, :, 128:256]
                            adjust = jnp.tanh(one * two) * avs[c] + one * bvs[c]
                            first, second = new[:, 0:128] + adjust, new[:, 128:256] - adjust
                            s0[c, :, 0:128] = first
                            s0[c, :, 128:256] = second
                            xs[c, :, 0:128] = first.astype(BF16)
                            xs[c, :, 128:256] = second.astype(BF16)
                        else:
                            xs[c] = new.astype(BF16)
            return carry

        lax.fori_loop(0, NSUB, substep, 0, unroll=UNROLL)

        mean = jnp.zeros((PER * 64, 128), F32)
        for t in range(3):
            diff = (xs[t * PER : t * PER + PER] - x0[t * PER : t * PER + PER]).reshape(PER * 64, 256)
            mean += _dot(diff, gather[t * 256 : t * 256 + 256, :])
        total = mean[0:64]
        for p in range(1, PER):
            total += pltpu.roll(mean[64 * p : 64 * p + 64], 16 * p, 1)
        tend = _dot(jnp.transpose(total), tg[...], precision=HIGHEST)
        for p in range(PER):
            for r in range(2):
                row = 16 * p + 8 * r
                tbuf[dests[p], r] = tend[row : row + 8]
                home = pl.ds(order[r, dests[p], 0], 1)
                updf[2 * p + r : 2 * p + r + 1, :] = tend[row : row + 1] + trt[r, home, :]
        usend[ch] = updf[...].astype(BF16)

        for p in range(PER):
            k = ch * PER + p
            one, two = s0[p, :, 0:128], s0[p, :, 128:256]
            left = jnp.where(low64, one, pltpu.roll(two, 64, 1)).astype(BF16)
            right = jnp.where(low64, pltpu.roll(one, 64, 1), two).astype(BF16)
            snd[k, _part(0, 0), :] = left[0:58]
            snd[k, _part(1, 0), :] = right[0:58]
            for t in (1, 2):
                for r in range(2):
                    snd[k, _part(r, t), :] = xs[t * PER + p, 0:58, 128 * r : 128 * r + 128]

        @pl.when(ch == 0)
        def _():
            pl.semaphore_wait(barrier, NBLK - 1)
            for k in range(NBLK - 1):
                pack_copy(k).start()

        for k in range(NBLK - 1):
            tracer_copy(ch, k).start()
        own_tracer(ch).start()
        for j in range(PER - 1):
            state_copy(ch * PER + j, dests[j]).start()

        @pl.when(ch < CHUNKS - 1)
        def _():
            state_copy(ch * PER + PER - 1, dests[PER - 1]).start()

        return carry

    lax.fori_loop(0, CHUNKS, chunk, 0)

    own_state = pltpu.make_async_copy(snd.at[NBLK - 1], recv.at[me], self_sem)
    own_state.start()
    tend_copy = pltpu.make_async_copy(tbuf, tend_out, tend_sem)
    tend_copy.start()

    tend_copy.wait()
    own_state.wait()
    own_pack.wait()
    for ch in range(CHUNKS):
        own_tracer(ch).wait()
    for k in range(NBLK - 1):
        pack_copy(k).wait()
        state_copy(k, peers[k]).wait()
        for ch in range(CHUNKS):
            tracer_copy(ch, k).wait()


def place(
    plan_s,
    recv,
    trec_hbm,
    prec_hbm,
    tbuf_hbm,
    shift,
    frac,
    state_out,
    tend_out,
    polar_out,
    prec,
    tbuf,
    trec,
    tend_v,
    polar_v,
    rbuf,
    wide,
    obuf,
    tn,
    slots_v,
    slots_s,
    loop,
    cs,
    cf,
    small_sem,
    in_sem,
    slot_sem,
    out_sem,
):
    me = lax.axis_index("lon")
    smalls = [
        pltpu.make_async_copy(src, dst, small_sem.at[n])
        for n, (src, dst) in enumerate(((prec_hbm, prec), (tbuf_hbm, tbuf), (trec_hbm, trec)))
    ]
    loads = [
        pltpu.make_async_copy(recv.at[pl.ds(8 * q, 8)], rbuf.at[pl.ds(8 * q, 8)], in_sem.at[q])
        for q in range(4)
    ]
    for load in smalls + loads:
        load.start()
    smalls[0].wait()
    plans = prec[...]
    held = (plans // 32 == me) & (_iota((32, 8, 128), 2) < 32) & (_iota((32, 8, 128), 1) < 2)
    mine = jnp.where(held, plans % 32, 0)
    slots_v[...] = jnp.broadcast_to(jnp.max(mine, axis=2, keepdims=True), (32, 8, 128))
    to_smem = pltpu.make_async_copy(slots_v, slots_s, slot_sem)
    to_smem.start()
    smalls[1].wait()

    for r in range(2):
        for i in range(32):
            tn[pl.ds(r * 6 * STEP + i, 6, stride=STEP), :] = tbuf[plan_s[r, i] // 32, r, 0:6, :]
        for f in range(6):
            at = (r * 6 + f) * STEP
            tend_v[r, f] = tn[at : at + 32, 0:72]
    outs = [pltpu.make_async_copy(tend_v, tend_out, out_sem.at[4])]
    outs[0].start()

    smalls[2].wait()
    target = _iota((64, 64), 0)
    for s in range(32):
        spots = jnp.broadcast_to(prec[s, 2:3, 0:64], (64, 64))
        rows = _dot(_onehot(spots == target), trec[s].reshape(64, 128))
        for r in range(2):
            loop[r, 32 * s : 32 * s + 32, :] = rows[32 * r : 32 * r + 32]

    cs[...] = jnp.zeros_like(cs)
    cf[...] = jnp.zeros_like(cf)
    cs[0:2, 0:72] = shift[...]
    cf[0:2, 0:72] = frac[...]
    for r in range(2):
        base = (me * 32 - 1 - cs[r : r + 1, :]) & 1023
        whole = loop[r]
        cut = jnp.concatenate([whole[512:1024], whole[0:32]], axis=0)
        now = jnp.where((base & 512) != 0, cut, whole[0:544])
        for size in (256, 128, 64, 32, 16, 8):
            rows = size + 32
            now = jnp.where((base & size) != 0, now[size : size + rows], now[0:rows])
        for size in (4, 2, 1):
            now = jnp.where((base & size) != 0, pltpu.roll(now, 40 - size, 0), now)
        weight = cf[r : r + 1, :]
        result = (1.0 - weight) * pltpu.roll(now, 39, 0) + weight * now
        polar_v[r] = result[0:32, 0:72]
    outs.append(pltpu.make_async_copy(polar_v, polar_out, out_sem.at[5]))
    outs[1].start()

    to_smem.wait()
    for q in range(4):
        loads[q].wait()

        def spot(s, carry):
            for r in range(2):
                at = pl.ds(r * 58 * STEP + slots_s[s, r, 0], 58, stride=STEP)
                for t in range(3):
                    wide[t, at, :] = rbuf[s, _part(r, t), :].astype(F32)
            return carry

        lax.fori_loop(8 * q, 8 * q + 8, spot, 0, unroll=2)

    for r in range(2):
        for part in range(2):

            def narrow(level, carry):
                for t in range(3):
                    obuf[r, level, :, 128 * t : 128 * t + 128] = wide[
                        t, pl.ds((r * 58 + level) * STEP, 32), :
                    ].astype(BF16)
                return carry

            lax.fori_loop(29 * part, 29 * part + 29, narrow, 0, unroll=True)
            piece = pl.ds(29 * part, 29)
            outs.append(
                pltpu.make_async_copy(
                    obuf.at[r, piece], state_out.at[r, piece], out_sem.at[2 * r + part]
                )
            )
            outs[-1].start()
    for out in outs:
        out.wait()


def per_device(
    crm_state,
    gcm_state,
    micro_flags,
    load_plan,
    h_mix,
    v_mix,
    to_crm,
    to_gcm,
    polar_tracer,
    courant_shift,
    courant_frac,
):
    smem = pl.BlockSpec(memory_space=pltpu.SMEM)
    vmem = pl.BlockSpec(memory_space=pltpu.VMEM)
    hbm = pl.BlockSpec(memory_space=pl.ANY)
    dma = pltpu.SemaphoreType.DMA
    recv, trec, prec, tbuf = pl.pallas_call(
        advance,
        out_shape=(
            jax.ShapeDtypeStruct((32, 348, 128), BF16),
            jax.ShapeDtypeStruct((32, CHUNKS, 2 * PER, 128), BF16),
            jax.ShapeDtypeStruct((32, 8, 128), jnp.int32),
            jax.ShapeDtypeStruct((32, 2, 8, 128), F32),
        ),
        in_specs=[smem, vmem, hbm] + [vmem] * 6,
        out_specs=(hbm, hbm, hbm, hbm),
        scratch_shapes=[
            pltpu.VMEM((32, 2, 8, 128), F32),
            pltpu.VMEM((2, 58, 32, 384), BF16),
            pltpu.VMEM((3, 2 * 58 * STEP, 128), F32),
            pltpu.VMEM((3 * PER, 64, 256), BF16),
            pltpu.VMEM((3 * PER, 64, 256), BF16),
            pltpu.VMEM((PER, 64, 256), F32),
            pltpu.VMEM((3 * PER, 64, 256), F32),
            pltpu.VMEM((PER, 64, 256), BF16),
            pltpu.VMEM((2 * 6 * STEP, 128), F32),
            pltpu.VMEM((128, 128), F32),
            pltpu.VMEM((256, 256), BF16),
            pltpu.VMEM((256, 256), BF16),
            pltpu.VMEM((3, 256, 256), BF16),
            pltpu.VMEM((768, 128), BF16),
            pltpu.VMEM((64, 128), F32),
            pltpu.VMEM((64, 128), F32),
            pltpu.VMEM((2, 32, 128), F32),
            pltpu.VMEM((2 * PER, 128), F32),
            pltpu.VMEM((CHUNKS, 2 * PER, 128), BF16),
            pltpu.VMEM((32, 348, 128), BF16),
            pltpu.VMEM((8, 128), jnp.int32),
            pltpu.VMEM((2, 32, 128), jnp.int32),
            pltpu.SMEM((2, 32, 128), jnp.int32),
            dma((2,)),
            dma,
            dma,
            dma,
            dma((NBLK,)),
            dma((NBLK,)),
            dma((NBLK,)),
            dma((NBLK,)),
            dma((CHUNKS, NBLK)),
            dma((CHUNKS, NBLK)),
        ],
        compiler_params=pltpu.CompilerParams(collective_id=0, has_side_effects=True),
        name="advance",
    )(
        micro_flags,
        load_plan,
        jnp.transpose(crm_state, (0, 2, 1, 3)),
        jnp.transpose(gcm_state, (0, 2, 1, 3)),
        h_mix,
        v_mix,
        to_crm,
        to_gcm.T,
        jnp.transpose(polar_tracer, (0, 2, 1)),
    )
    new_state, tendency, polar_next = pl.pallas_call(
        place,
        out_shape=(
            jax.ShapeDtypeStruct((2, 58, 32, 384), BF16),
            jax.ShapeDtypeStruct((2, 6, 32, 72), F32),
            jax.ShapeDtypeStruct((2, 32, 72), F32),
        ),
        in_specs=[smem] + [hbm] * 4 + [vmem] * 2,
        out_specs=(hbm, hbm, hbm),
        scratch_shapes=[
            pltpu.VMEM((32, 8, 128), jnp.int32),
            pltpu.VMEM((32, 2, 8, 128), F32),
            pltpu.VMEM((32, CHUNKS, 2 * PER, 128), BF16),
            pltpu.VMEM((2, 6, 32, 72), F32),
            pltpu.VMEM((2, 32, 72), F32),
            pltpu.VMEM((32, 348, 128), BF16),
            pltpu.VMEM((3, 2 * 58 * STEP, 128), F32),
            pltpu.VMEM((2, 58, 32, 384), BF16),
            pltpu.VMEM((2 * 6 * STEP, 128), F32),
            pltpu.VMEM((32, 8, 128), jnp.int32),
            pltpu.SMEM((32, 8, 128), jnp.int32),
            pltpu.VMEM((2, 1024, 128), F32),
            pltpu.VMEM((8, 128), jnp.int32),
            pltpu.VMEM((8, 128), F32),
            dma((3,)),
            dma((4,)),
            dma,
            dma((6,)),
        ],
        name="place",
    )(load_plan, recv, trec, prec, tbuf, courant_shift, courant_frac)
    return (
        jnp.transpose(new_state, (0, 2, 1, 3)),
        jnp.transpose(tendency, (0, 2, 1, 3)),
        jnp.transpose(polar_next, (0, 2, 1)),
    )


def solution(mesh):
    in_specs = (
        P("lat", "lon", None, None),
        P("lat", "lon", None, None),
        P("lat", "lon"),
        P("lat", "lon"),
        P(),
        P(),
        P(),
        P(),
        P("lat", None, "lon"),
        P("lat", None),
        P("lat", None),
    )
    out_specs = (P("lat", "lon", None, None), P("lat", "lon", None, None), P("lat", None, "lon"))
    return jax.shard_map(
        per_device, mesh=mesh, in_specs=in_specs, out_specs=out_specs, check_vma=False
    )
```

```python
import functools

import jax
import jax.numpy as jnp
from jax import lax
from jax.experimental import pallas as pl
from jax.experimental.pallas import tpu as pltpu
from jax.sharding import PartitionSpec as P

NSUB = 18
MESH = pl.DeviceIdType.MESH
F32 = jnp.float32
BF16 = jnp.bfloat16
HIGHEST = lax.Precision.HIGHEST

SIZES = (4, 4, 2)


def _hops(off):
    return sum(min(d, n - d) for d, n in zip(off, SIZES))


OFFSETS = sorted(
    ((a, b, c) for a in range(4) for b in range(4) for c in range(2)),
    key=lambda off: (-_hops(off), off),
)
NEAR = [(1, 1, 0), (3, 3, 0), (1, 0, 0), (3, 0, 0), (0, 1, 0), (0, 3, 0), (0, 0, 1), (0, 0, 0)]
OFFSETS = [off for off in OFFSETS if off not in NEAR] + NEAR
NBLK = len(OFFSETS)
CHUNKS = 4
PER = NBLK // CHUNKS
GROUPS = ((0, 8, 1, 9), (2, 3, 10, 11), (4, 5, 12, 13))
UNROLL = 18
MERGE = 3
STEP = 33


def _shifted(me, off):
    x, z, y = me // 8, (me // 2) % 4, me % 2
    return ((x + off[0]) % 4) * 8 + ((z + off[1]) % 4) * 2 + (y + off[2]) % 2


def _pick(index, values):
    out = jnp.int32(values[0])
    for i, value in enumerate(values[1:], 1):
        out = jnp.where(index == i, jnp.int32(value), out)
    return out


def _iota(shape, axis):
    return lax.broadcasted_iota(jnp.int32, shape, axis)


def _dot(a, b, **kw):
    return jnp.dot(a, b, preferred_element_type=F32, **kw)


def _onehot(mask):
    return jnp.where(mask, jnp.float32(1), jnp.float32(0)).astype(BF16)


def _part(r, t):
    return slice(58 * (3 * r + t), 58 * (3 * r + t) + 58)


def _lane_map(quarter, lanes):
    out = jnp.full(quarter.shape, lanes[0], jnp.int32)
    for i, lane in enumerate(lanes[1:], 1):
        out = jnp.where(quarter == i, lane, out)
    return out


def advance(
    flags,
    plan_v,
    crm,
    gcm,
    h_ref,
    v_ref,
    to_crm,
    to_gcm,
    tracer,
    recv,
    trec,
    prec,
    tend_out,
    tbuf,
    cn,
    xs,
    x0,
    s0,
    fs,
    lf,
    gn,
    gsc,
    hbd,
    vbd,
    spread,
    gather,
    tc,
    tg,
    trt,
    updf,
    usend,
    snd,
    pack,
    order_v,
    order,
    order_sem,
    self_sem,
    tend_sem,
    ssem,
    rsem,
    pssem,
    prsem,
    tssem,
    trsem,
):
    me = lax.axis_index("lon")

    peers = [_shifted(me, off) for off in OFFSETS]
    barrier = pltpu.get_barrier_semaphore()
    for k in range(NBLK - 1):
        pl.semaphore_signal(barrier, inc=1, device_id={"lon": peers[k]}, device_id_type=MESH)

    for r in range(2):
        owners = jnp.broadcast_to(plan_v[r : r + 1, :] // 32, (32, 32))
        at = jnp.where(owners == _iota((32, 32), 0), _iota((32, 32), 1), 0)
        order_v[r] = jnp.broadcast_to(jnp.max(at, axis=1, keepdims=True), (32, 128))
    lane = _iota((1, 128), 1)
    bound = jnp.full((1, 128), 64, jnp.int32)
    for k in range(NBLK):
        bound = jnp.where(lane // 2 == k, peers[k], bound)
    value = jnp.where(_iota((32, 128), 1) % 2 == 0, order_v[0], order_v[1] + 32)
    spot = jnp.where(bound == _iota((32, 128), 0), value, 0)
    pack[...] = jnp.zeros_like(pack)
    pack[0:2, 0:32] = plan_v[...]
    pack[2:3, :] = jnp.max(spot, axis=0, keepdims=True)
    to_smem = pltpu.make_async_copy(order_v, order, order_sem)
    to_smem.start()

    tile_h = _onehot(_iota((64, 256), 1) % 64 == _iota((64, 256), 0))
    tile_ht = _onehot(_iota((256, 64), 0) % 64 == _iota((256, 64), 1))
    tile_v = _onehot(_iota((58, 256), 1) % 64 == _iota((58, 256), 0))
    tile_vt = _onehot(_iota((256, 58), 0) % 64 == _iota((256, 58), 1))
    diag = _iota((256, 256), 0) // 64 == _iota((256, 256), 1) // 64
    h_rep = _dot(_dot(tile_ht, h_ref[...]).astype(BF16), tile_h)
    v_rep = _dot(_dot(tile_vt, v_ref[...]).astype(BF16), tile_v)
    hbd[...] = jnp.where(diag, h_rep, 0.0).astype(BF16)
    vbd[...] = jnp.where(diag, v_rep, 0.0).astype(BF16)
    for t, lanes in enumerate(GROUPS):
        spread[t] = _onehot(_iota((256, 256), 0) % 128 == _lane_map(_iota((256, 256), 1) // 64, lanes))
        hit = _iota((256, 128), 1) == _lane_map(_iota((256, 128), 0) // 64, lanes)
        gather[t * 256 : t * 256 + 256, :] = jnp.where(hit, jnp.float32(1.0 / 64), 0.0).astype(BF16)
    tc[...] = jnp.zeros_like(tc)
    tc[0:58, 0:72] = 0.5 * to_crm[...]
    tg[...] = jnp.zeros_like(tg)
    tg[0:58, 0:72] = to_gcm[...]
    gsc[...] = jnp.zeros_like(gsc)
    gn[...] = jnp.zeros_like(gn)
    xs[...] = jnp.zeros_like(xs)
    x0[...] = jnp.zeros_like(x0)
    s0[...] = jnp.zeros_like(s0)
    trt[...] = jnp.zeros_like(trt)
    for r in range(2):
        trt[r, :, 0:72] = tracer[r]
        for f in range(6):
            gn[(r * 6 + f) * STEP : (r * 6 + f) * STEP + 32, 0:72] = gcm[r, f].astype(F32)

    for r in range(2):

        def widen(level, carry):
            block = crm[r, level].astype(F32)
            for t in range(3):
                cn[t, pl.ds((r * 58 + level) * STEP, 32), :] = block[:, 128 * t : 128 * t + 128]
            return carry

        lax.fori_loop(0, 58, widen, 0, unroll=2)
    to_smem.wait()

    def pack_copy(k):
        return pltpu.make_async_remote_copy(
            src_ref=pack,
            dst_ref=prec.at[me],
            send_sem=pssem.at[k],
            recv_sem=prsem.at[k],
            device_id={"lon": peers[k]},
            device_id_type=MESH,
        )

    own_pack = pltpu.make_async_copy(pack, prec.at[me], pssem.at[NBLK - 1])
    own_pack.start()

    def tracer_copy(ch, k):
        return pltpu.make_async_remote_copy(
            src_ref=usend.at[ch],
            dst_ref=trec.at[me, ch],
            send_sem=tssem.at[ch, k],
            recv_sem=trsem.at[ch, k],
            device_id={"lon": peers[k]},
            device_id_type=MESH,
        )

    def own_tracer(ch):
        return pltpu.make_async_copy(usend.at[ch], trec.at[me, ch], tssem.at[ch, NBLK - 1])

    low58 = _iota((58, 128), 1) < 64
    low64 = _iota((64, 128), 1) < 64
    low1 = _iota((1, 128), 1) < 64

    def state_copy(k, dest):
        return pltpu.make_async_remote_copy(
            src_ref=snd.at[k],
            dst_ref=recv.at[me],
            send_sem=ssem.at[k],
            recv_sem=rsem.at[k],
            device_id={"lon": dest},
            device_id_type=MESH,
        )

    def chunk(ch, carry):
        dests = []
        for j in range(PER):
            offs = [OFFSETS[c * PER + j] for c in range(CHUNKS)]
            off = [_pick(ch, [o[i] for o in offs]) for i in range(3)]
            dests.append(_shifted(me, off))
        avs, bvs = [], []
        for p in range(PER):
            cols, a, b = [], [], []
            for r in range(2):
                i = order[r, dests[p], 0]
                cols.append([cn[t, pl.ds(r * 58 * STEP + i, 58, stride=STEP), :] for t in range(3)])
                row = 16 * p + 8 * r
                gsc[row : row + 6, :] = gn[pl.ds(r * 6 * STEP + i, 6, stride=STEP), :]
                flag = flags[r, i]
                a.append(jnp.where(flag == 1, jnp.float32(0.5), jnp.float32(0)))
                b.append(jnp.where(flag == 1, jnp.float32(0), jnp.float32(-0.25)))
            avs.append(jnp.where(low1, a[0], a[1]))
            bvs.append(jnp.where(low1, b[0], b[1]))
            one, two = cols[0][0], cols[1][0]
            first = jnp.where(low58, one, pltpu.roll(two, 64, 1))
            second = jnp.where(low58, pltpu.roll(one, 64, 1), two)
            s0[p, 0:58, 0:128] = first
            s0[p, 0:58, 128:256] = second
            blocks = ((first, second), (cols[0][1], cols[1][1]), (cols[0][2], cols[1][2]))
            for t in range(3):
                for half in range(2):
                    narrow = blocks[t][half].astype(BF16)
                    xs[t * PER + p, 0:58, 128 * half : 128 * half + 128] = narrow
                    x0[t * PER + p, 0:58, 128 * half : 128 * half + 128] = narrow
        forcing = lax.dot_general(
            tc[...],
            gsc[...],
            (((1,), (1,)), ((), ())),
            precision=HIGHEST,
            preferred_element_type=F32,
        )
        for p in range(PER):
            turned = forcing if p == 0 else pltpu.roll(forcing, 128 - 16 * p, 1)
            hi = turned.astype(BF16)
            lf[p, :, 0:128] = hi
            lf[p, :, 128:256] = (turned - hi.astype(F32)).astype(BF16)
        both = lf[...].reshape(PER * 64, 256)
        for t in range(3):
            fs[t * PER : t * PER + PER] = _dot(both, spread[t]).reshape(PER, 64, 256)

        def substep(step, carry):
            h, v = hbd[...], vbd[...]
            for m in range(0, 3 * PER // 4, MERGE):
                x = xs[4 * m : 4 * (m + MERGE)].reshape(MERGE * 256, 256)
                all_mixed = _dot(x, h).astype(BF16)
                for q in range(m, m + MERGE):
                    mixed = all_mixed[256 * (q - m) : 256 * (q - m) + 256]
                    grown = jnp.tanh(_dot(v, mixed))
                    for i in range(4):
                        c = 4 * q + i
                        new = grown[64 * i : 64 * i + 64] + fs[c]
                        if c < PER:
                            one, two = s0[c, :, 0:128], s0[c, :, 128:256]
                            adjust = jnp.tanh(one * two) * avs[c] + one * bvs[c]
                            first, second = new[:, 0:128] + adjust, new[:, 128:256] - adjust
                            s0[c, :, 0:128] = first
                            s0[c, :, 128:256] = second
                            xs[c, :, 0:128] = first.astype(BF16)
                            xs[c, :, 128:256] = second.astype(BF16)
                        else:
                            xs[c] = new.astype(BF16)
            return carry

        lax.fori_loop(0, NSUB, substep, 0, unroll=UNROLL)

        mean = jnp.zeros((PER * 64, 128), F32)
        for t in range(3):
            diff = (xs[t * PER : t * PER + PER] - x0[t * PER : t * PER + PER]).reshape(PER * 64, 256)
            mean += _dot(diff, gather[t * 256 : t * 256 + 256, :])
        total = mean[0:64]
        for p in range(1, PER):
            total += pltpu.roll(mean[64 * p : 64 * p + 64], 16 * p, 1)
        tend = _dot(jnp.transpose(total), tg[...], precision=HIGHEST)
        for p in range(PER):
            for r in range(2):
                row = 16 * p + 8 * r
                tbuf[dests[p], r] = tend[row : row + 8]
                home = pl.ds(order[r, dests[p], 0], 1)
                updf[2 * p + r : 2 * p + r + 1, :] = tend[row : row + 1] + trt[r, home, :]
        usend[ch] = updf[...].astype(BF16)

        for p in range(PER):
            k = ch * PER + p
            one, two = s0[p, :, 0:128], s0[p, :, 128:256]
            left = jnp.where(low64, one, pltpu.roll(two, 64, 1)).astype(BF16)
            right = jnp.where(low64, pltpu.roll(one, 64, 1), two).astype(BF16)
            snd[k, _part(0, 0), :] = left[0:58]
            snd[k, _part(1, 0), :] = right[0:58]
            for t in (1, 2):
                for r in range(2):
                    snd[k, _part(r, t), :] = xs[t * PER + p, 0:58, 128 * r : 128 * r + 128]

        @pl.when(ch == 0)
        def _():
            pl.semaphore_wait(barrier, NBLK - 1)
            for k in range(NBLK - 1):
                pack_copy(k).start()

        for k in range(NBLK - 1):
            tracer_copy(ch, k).start()
        own_tracer(ch).start()
        for j in range(PER - 1):
            state_copy(ch * PER + j, dests[j]).start()

        @pl.when(ch < CHUNKS - 1)
        def _():
            state_copy(ch * PER + PER - 1, dests[PER - 1]).start()

        return carry

    lax.fori_loop(0, CHUNKS, chunk, 0)

    own_state = pltpu.make_async_copy(snd.at[NBLK - 1], recv.at[me], self_sem)
    own_state.start()
    tend_copy = pltpu.make_async_copy(tbuf, tend_out, tend_sem)
    tend_copy.start()

    tend_copy.wait()
    own_state.wait()
    own_pack.wait()
    for ch in range(CHUNKS):
        own_tracer(ch).wait()
    for k in range(NBLK - 1):
        pack_copy(k).wait()
        state_copy(k, peers[k]).wait()
        for ch in range(CHUNKS):
            tracer_copy(ch, k).wait()


def place(
    plan_s,
    recv,
    trec,
    prec,
    tbuf,
    shift,
    frac,
    state_out,
    tend_out,
    polar_out,
    tend_v,
    polar_v,
    wide,
    obuf,
    tn,
    slots_v,
    slots_s,
    loop,
    cs,
    cf,
    slot_sem,
    out_sem,
):
    me = lax.axis_index("lon")
    plans = prec[...]
    held = (plans // 32 == me) & (_iota((32, 8, 128), 2) < 32) & (_iota((32, 8, 128), 1) < 2)
    mine = jnp.where(held, plans % 32, 0)
    slots_v[...] = jnp.broadcast_to(jnp.max(mine, axis=2, keepdims=True), (32, 8, 128))
    to_smem = pltpu.make_async_copy(slots_v, slots_s, slot_sem)
    to_smem.start()

    for r in range(2):
        for i in range(32):
            tn[pl.ds(r * 6 * STEP + i, 6, stride=STEP), :] = tbuf[plan_s[r, i] // 32, r, 0:6, :]
        for f in range(6):
            at = (r * 6 + f) * STEP
            tend_v[r, f] = tn[at : at + 32, 0:72]
    outs = [pltpu.make_async_copy(tend_v, tend_out, out_sem.at[4])]
    outs[0].start()

    target = _iota((64, 64), 0)
    for s in range(32):
        spots = jnp.broadcast_to(prec[s, 2:3, 0:64], (64, 64))
        rows = _dot(_onehot(spots == target), trec[s].reshape(64, 128))
        for r in range(2):
            loop[r, 32 * s : 32 * s + 32, :] = rows[32 * r : 32 * r + 32]

    cs[...] = jnp.zeros_like(cs)
    cf[...] = jnp.zeros_like(cf)
    cs[0:2, 0:72] = shift[...]
    cf[0:2, 0:72] = frac[...]
    for r in range(2):
        base = (me * 32 - 1 - cs[r : r + 1, :]) & 1023
        whole = loop[r]
        cut = jnp.concatenate([whole[512:1024], whole[0:32]], axis=0)
        now = jnp.where((base & 512) != 0, cut, whole[0:544])
        for size in (256, 128, 64, 32, 16, 8):
            rows = size + 32
            now = jnp.where((base & size) != 0, now[size : size + rows], now[0:rows])
        for size in (4, 2, 1):
            now = jnp.where((base & size) != 0, pltpu.roll(now, 40 - size, 0), now)
        weight = cf[r : r + 1, :]
        result = (1.0 - weight) * pltpu.roll(now, 39, 0) + weight * now
        polar_v[r] = result[0:32, 0:72]
    outs.append(pltpu.make_async_copy(polar_v, polar_out, out_sem.at[5]))
    outs[1].start()

    to_smem.wait()
    for q in range(4):

        def spot(s, carry):
            for r in range(2):
                at = pl.ds(r * 58 * STEP + slots_s[s, r, 0], 58, stride=STEP)
                for t in range(3):
                    wide[t, at, :] = recv[s, _part(r, t), :].astype(F32)
            return carry

        lax.fori_loop(8 * q, 8 * q + 8, spot, 0, unroll=2)

    for r in range(2):
        for part in range(2):

            def narrow(level, carry):
                for t in range(3):
                    obuf[r, level, :, 128 * t : 128 * t + 128] = wide[
                        t, pl.ds((r * 58 + level) * STEP, 32), :
                    ].astype(BF16)
                return carry

            lax.fori_loop(29 * part, 29 * part + 29, narrow, 0, unroll=True)
            piece = pl.ds(29 * part, 29)
            outs.append(
                pltpu.make_async_copy(
                    obuf.at[r, piece], state_out.at[r, piece], out_sem.at[2 * r + part]
                )
            )
            outs[-1].start()
    for out in outs:
        out.wait()


def per_device(
    crm_state,
    gcm_state,
    micro_flags,
    load_plan,
    h_mix,
    v_mix,
    to_crm,
    to_gcm,
    polar_tracer,
    courant_shift,
    courant_frac,
):
    smem = pl.BlockSpec(memory_space=pltpu.SMEM)
    vmem = pl.BlockSpec(memory_space=pltpu.VMEM)
    hbm = pl.BlockSpec(memory_space=pl.ANY)
    dma = pltpu.SemaphoreType.DMA
    recv, trec, prec, tbuf = pl.pallas_call(
        advance,
        out_shape=(
            jax.ShapeDtypeStruct((32, 348, 128), BF16),
            jax.ShapeDtypeStruct((32, CHUNKS, 2 * PER, 128), BF16),
            jax.ShapeDtypeStruct((32, 8, 128), jnp.int32),
            jax.ShapeDtypeStruct((32, 2, 8, 128), F32),
        ),
        in_specs=[smem] + [vmem] * 8,
        out_specs=(hbm, hbm, hbm, hbm),
        scratch_shapes=[
            pltpu.VMEM((32, 2, 8, 128), F32),
            pltpu.VMEM((3, 2 * 58 * STEP, 128), F32),
            pltpu.VMEM((3 * PER, 64, 256), BF16),
            pltpu.VMEM((3 * PER, 64, 256), BF16),
            pltpu.VMEM((PER, 64, 256), F32),
            pltpu.VMEM((3 * PER, 64, 256), F32),
            pltpu.VMEM((PER, 64, 256), BF16),
            pltpu.VMEM((2 * 6 * STEP, 128), F32),
            pltpu.VMEM((128, 128), F32),
            pltpu.VMEM((256, 256), BF16),
            pltpu.VMEM((256, 256), BF16),
            pltpu.VMEM((3, 256, 256), BF16),
            pltpu.VMEM((768, 128), BF16),
            pltpu.VMEM((64, 128), F32),
            pltpu.VMEM((64, 128), F32),
            pltpu.VMEM((2, 32, 128), F32),
            pltpu.VMEM((2 * PER, 128), F32),
            pltpu.VMEM((CHUNKS, 2 * PER, 128), BF16),
            pltpu.VMEM((32, 348, 128), BF16),
            pltpu.VMEM((8, 128), jnp.int32),
            pltpu.VMEM((2, 32, 128), jnp.int32),
            pltpu.SMEM((2, 32, 128), jnp.int32),
            dma,
            dma,
            dma,
            dma((NBLK,)),
            dma((NBLK,)),
            dma((NBLK,)),
            dma((NBLK,)),
            dma((CHUNKS, NBLK)),
            dma((CHUNKS, NBLK)),
        ],
        compiler_params=pltpu.CompilerParams(
            collective_id=0, has_side_effects=True, vmem_limit_bytes=26 << 20
        ),
        name="advance",
    )(
        micro_flags,
        load_plan,
        jnp.transpose(crm_state, (0, 2, 1, 3)),
        jnp.transpose(gcm_state, (0, 2, 1, 3)),
        h_mix,
        v_mix,
        to_crm,
        to_gcm.T,
        jnp.transpose(polar_tracer, (0, 2, 1)),
    )
    new_state, tendency, polar_next = pl.pallas_call(
        place,
        out_shape=(
            jax.ShapeDtypeStruct((2, 58, 32, 384), BF16),
            jax.ShapeDtypeStruct((2, 6, 32, 72), F32),
            jax.ShapeDtypeStruct((2, 32, 72), F32),
        ),
        in_specs=[smem] + [vmem] * 6,
        out_specs=(hbm, hbm, hbm),
        scratch_shapes=[
            pltpu.VMEM((2, 6, 32, 72), F32),
            pltpu.VMEM((2, 32, 72), F32),
            pltpu.VMEM((3, 2 * 58 * STEP, 128), F32),
            pltpu.VMEM((2, 58, 32, 384), BF16),
            pltpu.VMEM((2 * 6 * STEP, 128), F32),
            pltpu.VMEM((32, 8, 128), jnp.int32),
            pltpu.SMEM((32, 8, 128), jnp.int32),
            pltpu.VMEM((2, 1024, 128), F32),
            pltpu.VMEM((8, 128), jnp.int32),
            pltpu.VMEM((8, 128), F32),
            dma,
            dma((6,)),
        ],
        compiler_params=pltpu.CompilerParams(vmem_limit_bytes=24 << 20),
        name="place",
    )(load_plan, recv, trec, prec, tbuf, courant_shift, courant_frac)
    return (
        jnp.transpose(new_state, (0, 2, 1, 3)),
        jnp.transpose(tendency, (0, 2, 1, 3)),
        jnp.transpose(polar_next, (0, 2, 1)),
    )


def solution(mesh):
    in_specs = (
        P("lat", "lon", None, None),
        P("lat", "lon", None, None),
        P("lat", "lon"),
        P("lat", "lon"),
        P(),
        P(),
        P(),
        P(),
        P("lat", None, "lon"),
        P("lat", None),
        P("lat", None),
    )
    out_specs = (P("lat", "lon", None, None), P("lat", "lon", None, None), P("lat", None, "lon"))
    return jax.shard_map(
        per_device, mesh=mesh, in_specs=in_specs, out_specs=out_specs, check_vma=False
    )
```

```python
import functools

import jax
import jax.numpy as jnp
from jax import lax
from jax.experimental import pallas as pl
from jax.experimental.pallas import tpu as pltpu
from jax.sharding import PartitionSpec as P

NSUB = 18
MESH = pl.DeviceIdType.MESH
F32 = jnp.float32
BF16 = jnp.bfloat16
HIGHEST = lax.Precision.HIGHEST

SIZES = (4, 4, 2)


def _hops(off):
    return sum(min(d, n - d) for d, n in zip(off, SIZES))


OFFSETS = sorted(
    ((a, b, c) for a in range(4) for b in range(4) for c in range(2)),
    key=lambda off: (-_hops(off), off),
)
NEAR = [(1, 1, 0), (3, 3, 0), (1, 0, 0), (3, 0, 0), (0, 1, 0), (0, 3, 0), (0, 0, 1), (0, 0, 0)]
OFFSETS = [off for off in OFFSETS if off not in NEAR] + NEAR
NBLK = len(OFFSETS)
CHUNKS = 4
PER = NBLK // CHUNKS
GROUPS = ((0, 8, 1, 9), (2, 3, 10, 11), (4, 5, 12, 13))
UNROLL = 18
MERGE = 3
STEP = 33


def _shifted(me, off):
    x, z, y = me // 8, (me // 2) % 4, me % 2
    return ((x + off[0]) % 4) * 8 + ((z + off[1]) % 4) * 2 + (y + off[2]) % 2


def _pick(index, values):
    out = jnp.int32(values[0])
    for i, value in enumerate(values[1:], 1):
        out = jnp.where(index == i, jnp.int32(value), out)
    return out


def _iota(shape, axis):
    return lax.broadcasted_iota(jnp.int32, shape, axis)


def _dot(a, b, **kw):
    return jnp.dot(a, b, preferred_element_type=F32, **kw)


def _onehot(mask):
    return jnp.where(mask, jnp.float32(1), jnp.float32(0)).astype(BF16)


def _part(r, t):
    return slice(58 * (3 * r + t), 58 * (3 * r + t) + 58)


def _lane_map(quarter, lanes):
    out = jnp.full(quarter.shape, lanes[0], jnp.int32)
    for i, lane in enumerate(lanes[1:], 1):
        out = jnp.where(quarter == i, lane, out)
    return out


def advance(
    flags,
    plan_v,
    crm,
    gcm,
    h_ref,
    v_ref,
    to_crm,
    to_gcm,
    tracer,
    recv,
    trec,
    prec,
    tend_out,
    tbuf,
    crm_v,
    cn,
    xs,
    x0,
    s0,
    fs,
    lf,
    gn,
    gsc,
    hbd,
    vbd,
    spread,
    gather,
    tc,
    tg,
    trt,
    updf,
    usend,
    snd,
    pack,
    order_v,
    order,
    in_sem,
    order_sem,
    self_sem,
    tend_sem,
    ssem,
    rsem,
    pssem,
    prsem,
    tssem,
    trsem,
):
    me = lax.axis_index("lon")
    loads = [pltpu.make_async_copy(crm.at[r], crm_v.at[r], in_sem.at[r]) for r in range(2)]
    for load in loads:
        load.start()

    peers = [_shifted(me, off) for off in OFFSETS]
    barrier = pltpu.get_barrier_semaphore()
    for k in range(NBLK - 1):
        pl.semaphore_signal(barrier, inc=1, device_id={"lon": peers[k]}, device_id_type=MESH)

    for r in range(2):
        owners = jnp.broadcast_to(plan_v[r : r + 1, :] // 32, (32, 32))
        at = jnp.where(owners == _iota((32, 32), 0), _iota((32, 32), 1), 0)
        order_v[r] = jnp.broadcast_to(jnp.max(at, axis=1, keepdims=True), (32, 128))
    lane = _iota((1, 128), 1)
    bound = jnp.full((1, 128), 64, jnp.int32)
    for k in range(NBLK):
        bound = jnp.where(lane // 2 == k, peers[k], bound)
    value = jnp.where(_iota((32, 128), 1) % 2 == 0, order_v[0], order_v[1] + 32)
    spot = jnp.where(bound == _iota((32, 128), 0), value, 0)
    pack[...] = jnp.zeros_like(pack)
    pack[0:2, 0:32] = plan_v[...]
    pack[2:3, :] = jnp.max(spot, axis=0, keepdims=True)
    to_smem = pltpu.make_async_copy(order_v, order, order_sem)
    to_smem.start()

    tile_h = _onehot(_iota((64, 256), 1) % 64 == _iota((64, 256), 0))
    tile_ht = _onehot(_iota((256, 64), 0) % 64 == _iota((256, 64), 1))
    tile_v = _onehot(_iota((58, 256), 1) % 64 == _iota((58, 256), 0))
    tile_vt = _onehot(_iota((256, 58), 0) % 64 == _iota((256, 58), 1))
    diag = _iota((256, 256), 0) // 64 == _iota((256, 256), 1) // 64
    h_rep = _dot(_dot(tile_ht, h_ref[...]).astype(BF16), tile_h)
    v_rep = _dot(_dot(tile_vt, v_ref[...]).astype(BF16), tile_v)
    hbd[...] = jnp.where(diag, h_rep, 0.0).astype(BF16)
    vbd[...] = jnp.where(diag, v_rep, 0.0).astype(BF16)
    for t, lanes in enumerate(GROUPS):
        spread[t] = _onehot(_iota((256, 256), 0) % 128 == _lane_map(_iota((256, 256), 1) // 64, lanes))
        hit = _iota((256, 128), 1) == _lane_map(_iota((256, 128), 0) // 64, lanes)
        gather[t * 256 : t * 256 + 256, :] = jnp.where(hit, jnp.float32(1.0 / 64), 0.0).astype(BF16)
    tc[...] = jnp.zeros_like(tc)
    tc[0:58, 0:72] = 0.5 * to_crm[...]
    tg[...] = jnp.zeros_like(tg)
    tg[0:58, 0:72] = to_gcm[...]
    gsc[...] = jnp.zeros_like(gsc)
    gn[...] = jnp.zeros_like(gn)
    xs[:, 48:64, :] = jnp.zeros((3 * PER, 16, 256), BF16)
    x0[:, 48:64, :] = jnp.zeros((3 * PER, 16, 256), BF16)
    s0[:, 56:64, :] = jnp.zeros((PER, 8, 256), F32)
    trt[...] = jnp.zeros_like(trt)
    for r in range(2):
        trt[r, :, 0:72] = tracer[r]
        for f in range(6):
            gn[(r * 6 + f) * STEP : (r * 6 + f) * STEP + 32, 0:72] = gcm[r, f].astype(F32)

    for r in range(2):
        loads[r].wait()

        def widen(level, carry):
            block = crm_v[r, level].astype(F32)
            for t in range(3):
                cn[t, pl.ds((r * 58 + level) * STEP, 32), :] = block[:, 128 * t : 128 * t + 128]
            return carry

        lax.fori_loop(0, 58, widen, 0, unroll=2)
    to_smem.wait()

    def pack_copy(k):
        return pltpu.make_async_remote_copy(
            src_ref=pack,
            dst_ref=prec.at[me],
            send_sem=pssem.at[k],
            recv_sem=prsem.at[k],
            device_id={"lon": peers[k]},
            device_id_type=MESH,
        )

    own_pack = pltpu.make_async_copy(pack, prec.at[me], pssem.at[NBLK - 1])
    own_pack.start()

    def tracer_copy(ch, k):
        return pltpu.make_async_remote_copy(
            src_ref=usend.at[ch],
            dst_ref=trec.at[me, ch],
            send_sem=tssem.at[ch, k],
            recv_sem=trsem.at[ch, k],
            device_id={"lon": peers[k]},
            device_id_type=MESH,
        )

    def own_tracer(ch):
        return pltpu.make_async_copy(usend.at[ch], trec.at[me, ch], tssem.at[ch, NBLK - 1])

    low58 = _iota((58, 128), 1) < 64
    low64 = _iota((64, 128), 1) < 64
    low1 = _iota((1, 128), 1) < 64

    def state_copy(k, dest):
        return pltpu.make_async_remote_copy(
            src_ref=snd.at[k],
            dst_ref=recv.at[me],
            send_sem=ssem.at[k],
            recv_sem=rsem.at[k],
            device_id={"lon": dest},
            device_id_type=MESH,
        )

    def chunk(ch, carry):
        dests = []
        for j in range(PER):
            offs = [OFFSETS[c * PER + j] for c in range(CHUNKS)]
            off = [_pick(ch, [o[i] for o in offs]) for i in range(3)]
            dests.append(_shifted(me, off))
        avs, bvs = [], []
        for p in range(PER):
            cols, a, b = [], [], []
            for r in range(2):
                i = order[r, dests[p], 0]
                cols.append([cn[t, pl.ds(r * 58 * STEP + i, 58, stride=STEP), :] for t in range(3)])
                row = 16 * p + 8 * r
                gsc[row : row + 6, :] = gn[pl.ds(r * 6 * STEP + i, 6, stride=STEP), :]
                flag = flags[r, i]
                a.append(jnp.where(flag == 1, jnp.float32(0.5), jnp.float32(0)))
                b.append(jnp.where(flag == 1, jnp.float32(0), jnp.float32(-0.25)))
            avs.append(jnp.where(low1, a[0], a[1]))
            bvs.append(jnp.where(low1, b[0], b[1]))
            one, two = cols[0][0], cols[1][0]
            first = jnp.where(low58, one, pltpu.roll(two, 64, 1))
            second = jnp.where(low58, pltpu.roll(one, 64, 1), two)
            s0[p, 0:58, 0:128] = first
            s0[p, 0:58, 128:256] = second
            blocks = ((first, second), (cols[0][1], cols[1][1]), (cols[0][2], cols[1][2]))
            for t in range(3):
                for half in range(2):
                    narrow = blocks[t][half].astype(BF16)
                    xs[t * PER + p, 0:58, 128 * half : 128 * half + 128] = narrow
                    x0[t * PER + p, 0:58, 128 * half : 128 * half + 128] = narrow
        forcing = lax.dot_general(
            tc[...],
            gsc[...],
            (((1,), (1,)), ((), ())),
            precision=HIGHEST,
            preferred_element_type=F32,
        )
        for p in range(PER):
            turned = forcing if p == 0 else pltpu.roll(forcing, 128 - 16 * p, 1)
            hi = turned.astype(BF16)
            lf[p, :, 0:128] = hi
            lf[p, :, 128:256] = (turned - hi.astype(F32)).astype(BF16)
        both = lf[...].reshape(PER * 64, 256)
        for t in range(3):
            fs[t * PER : t * PER + PER] = _dot(both, spread[t]).reshape(PER, 64, 256)

        def substep(step, carry):
            h, v = hbd[...], vbd[...]
            for m in range(0, 3 * PER // 4, MERGE):
                x = xs[4 * m : 4 * (m + MERGE)].reshape(MERGE * 256, 256)
                all_mixed = _dot(x, h).astype(BF16)
                for q in range(m, m + MERGE):
                    mixed = all_mixed[256 * (q - m) : 256 * (q - m) + 256]
                    grown = jnp.tanh(_dot(v, mixed))
                    for i in range(4):
                        c = 4 * q + i
                        new = grown[64 * i : 64 * i + 64] + fs[c]
                        if c < PER:
                            one, two = s0[c, :, 0:128], s0[c, :, 128:256]
                            adjust = jnp.tanh(one * two) * avs[c] + one * bvs[c]
                            first, second = new[:, 0:128] + adjust, new[:, 128:256] - adjust
                            s0[c, :, 0:128] = first
                            s0[c, :, 128:256] = second
                            xs[c, :, 0:128] = first.astype(BF16)
                            xs[c, :, 128:256] = second.astype(BF16)
                        else:
                            xs[c] = new.astype(BF16)
            return carry

        lax.fori_loop(0, NSUB, substep, 0, unroll=UNROLL)

        mean = jnp.zeros((PER * 64, 128), F32)
        for t in range(3):
            diff = (xs[t * PER : t * PER + PER] - x0[t * PER : t * PER + PER]).reshape(PER * 64, 256)
            mean += _dot(diff, gather[t * 256 : t * 256 + 256, :])
        total = mean[0:64]
        for p in range(1, PER):
            total += pltpu.roll(mean[64 * p : 64 * p + 64], 16 * p, 1)
        tend = _dot(jnp.transpose(total), tg[...], precision=HIGHEST)
        for p in range(PER):
            for r in range(2):
                row = 16 * p + 8 * r
                tbuf[dests[p], r] = tend[row : row + 8]
                home = pl.ds(order[r, dests[p], 0], 1)
                updf[2 * p + r : 2 * p + r + 1, :] = tend[row : row + 1] + trt[r, home, :]
        usend[ch] = updf[...].astype(BF16)

        for p in range(PER):
            k = ch * PER + p
            one, two = s0[p, :, 0:128], s0[p, :, 128:256]
            left = jnp.where(low64, one, pltpu.roll(two, 64, 1)).astype(BF16)
            right = jnp.where(low64, pltpu.roll(one, 64, 1), two).astype(BF16)
            snd[k, _part(0, 0), :] = left[0:58]
            snd[k, _part(1, 0), :] = right[0:58]
            for t in (1, 2):
                for r in range(2):
                    snd[k, _part(r, t), :] = xs[t * PER + p, 0:58, 128 * r : 128 * r + 128]

        @pl.when(ch == 0)
        def _():
            pl.semaphore_wait(barrier, NBLK - 1)
            for k in range(NBLK - 1):
                pack_copy(k).start()

        for k in range(NBLK - 1):
            tracer_copy(ch, k).start()
        own_tracer(ch).start()
        for j in range(PER - 1):
            state_copy(ch * PER + j, dests[j]).start()

        @pl.when(ch < CHUNKS - 1)
        def _():
            state_copy(ch * PER + PER - 1, dests[PER - 1]).start()

        return carry

    lax.fori_loop(0, CHUNKS, chunk, 0)

    own_state = pltpu.make_async_copy(snd.at[NBLK - 1], recv.at[me], self_sem)
    own_state.start()
    tend_copy = pltpu.make_async_copy(tbuf, tend_out, tend_sem)
    tend_copy.start()

    tend_copy.wait()
    own_state.wait()
    own_pack.wait()
    for ch in range(CHUNKS):
        own_tracer(ch).wait()
    for k in range(NBLK - 1):
        pack_copy(k).wait()
        state_copy(k, peers[k]).wait()
        for ch in range(CHUNKS):
            tracer_copy(ch, k).wait()


def place(
    plan_s,
    recv,
    trec_hbm,
    prec_hbm,
    tbuf_hbm,
    shift,
    frac,
    state_out,
    tend_out,
    polar_out,
    prec,
    tbuf,
    trec,
    tend_v,
    polar_v,
    rbuf,
    wide,
    obuf,
    tn,
    slots_v,
    slots_s,
    loop,
    cs,
    cf,
    small_sem,
    in_sem,
    slot_sem,
    out_sem,
):
    me = lax.axis_index("lon")
    smalls = [
        pltpu.make_async_copy(src, dst, small_sem.at[n])
        for n, (src, dst) in enumerate(((prec_hbm, prec), (tbuf_hbm, tbuf), (trec_hbm, trec)))
    ]
    loads = [
        pltpu.make_async_copy(recv.at[pl.ds(8 * q, 8)], rbuf.at[pl.ds(8 * q, 8)], in_sem.at[q])
        for q in range(4)
    ]
    for load in smalls + loads:
        load.start()
    smalls[0].wait()
    plans = prec[...]
    held = (plans // 32 == me) & (_iota((32, 8, 128), 2) < 32) & (_iota((32, 8, 128), 1) < 2)
    mine = jnp.where(held, plans % 32, 0)
    slots_v[...] = jnp.broadcast_to(jnp.max(mine, axis=2, keepdims=True), (32, 8, 128))
    to_smem = pltpu.make_async_copy(slots_v, slots_s, slot_sem)
    to_smem.start()
    smalls[1].wait()

    for r in range(2):
        for i in range(32):
            tn[pl.ds(r * 6 * STEP + i, 6, stride=STEP), :] = tbuf[plan_s[r, i] // 32, r, 0:6, :]
        for f in range(6):
            at = (r * 6 + f) * STEP
            tend_v[r, f] = tn[at : at + 32, 0:72]
    outs = [pltpu.make_async_copy(tend_v, tend_out, out_sem.at[4])]
    outs[0].start()

    smalls[2].wait()
    target = _iota((64, 64), 0)
    for s in range(32):
        spots = jnp.broadcast_to(prec[s, 2:3, 0:64], (64, 64))
        rows = _dot(_onehot(spots == target), trec[s].reshape(64, 128))
        for r in range(2):
            loop[r, 32 * s : 32 * s + 32, :] = rows[32 * r : 32 * r + 32]

    to_smem.wait()
    for load in loads:
        load.wait()
    for r in range(2):

        def spot(s, carry):
            at = pl.ds(r * 58 * STEP + slots_s[s, r, 0], 58, stride=STEP)
            for t in range(3):
                wide[t, at, :] = rbuf[s, _part(r, t), :].astype(F32)
            return carry

        lax.fori_loop(0, 32, spot, 0, unroll=4)
        for part in range(2):
            for level in range(29 * part, 29 * part + 29):
                for t in range(3):
                    at = (r * 58 + level) * STEP
                    obuf[r, level, :, 128 * t : 128 * t + 128] = wide[t, at : at + 32, :].astype(BF16)
            piece = pl.ds(29 * part, 29)
            outs.append(
                pltpu.make_async_copy(
                    obuf.at[r, piece], state_out.at[r, piece], out_sem.at[2 * r + part]
                )
            )
            outs[-1].start()

    cs[...] = jnp.zeros_like(cs)
    cf[...] = jnp.zeros_like(cf)
    cs[0:2, 0:72] = shift[...]
    cf[0:2, 0:72] = frac[...]
    for r in range(2):
        base = (me * 32 - 1 - cs[r : r + 1, :]) & 1023
        whole = loop[r]
        cut = jnp.concatenate([whole[512:1024], whole[0:32]], axis=0)
        now = jnp.where((base & 512) != 0, cut, whole[0:544])
        for size in (256, 128, 64, 32, 16, 8):
            rows = size + 32
            now = jnp.where((base & size) != 0, now[size : size + rows], now[0:rows])
        for size in (4, 2, 1):
            now = jnp.where((base & size) != 0, pltpu.roll(now, 40 - size, 0), now)
        weight = cf[r : r + 1, :]
        result = (1.0 - weight) * pltpu.roll(now, 39, 0) + weight * now
        polar_v[r] = result[0:32, 0:72]
    outs.append(pltpu.make_async_copy(polar_v, polar_out, out_sem.at[5]))
    outs[-1].start()

    for out in outs:
        out.wait()


def per_device(
    crm_state,
    gcm_state,
    micro_flags,
    load_plan,
    h_mix,
    v_mix,
    to_crm,
    to_gcm,
    polar_tracer,
    courant_shift,
    courant_frac,
):
    smem = pl.BlockSpec(memory_space=pltpu.SMEM)
    vmem = pl.BlockSpec(memory_space=pltpu.VMEM)
    hbm = pl.BlockSpec(memory_space=pl.ANY)
    dma = pltpu.SemaphoreType.DMA
    recv, trec, prec, tbuf = pl.pallas_call(
        advance,
        out_shape=(
            jax.ShapeDtypeStruct((32, 348, 128), BF16),
            jax.ShapeDtypeStruct((32, CHUNKS, 2 * PER, 128), BF16),
            jax.ShapeDtypeStruct((32, 8, 128), jnp.int32),
            jax.ShapeDtypeStruct((32, 2, 8, 128), F32),
        ),
        in_specs=[smem, vmem, hbm] + [vmem] * 6,
        out_specs=(hbm, hbm, hbm, hbm),
        scratch_shapes=[
            pltpu.VMEM((32, 2, 8, 128), F32),
            pltpu.VMEM((2, 58, 32, 384), BF16),
            pltpu.VMEM((3, 2 * 58 * STEP, 128), F32),
            pltpu.VMEM((3 * PER, 64, 256), BF16),
            pltpu.VMEM((3 * PER, 64, 256), BF16),
            pltpu.VMEM((PER, 64, 256), F32),
            pltpu.VMEM((3 * PER, 64, 256), F32),
            pltpu.VMEM((PER, 64, 256), BF16),
            pltpu.VMEM((2 * 6 * STEP, 128), F32),
            pltpu.VMEM((128, 128), F32),
            pltpu.VMEM((256, 256), BF16),
            pltpu.VMEM((256, 256), BF16),
            pltpu.VMEM((3, 256, 256), BF16),
            pltpu.VMEM((768, 128), BF16),
            pltpu.VMEM((64, 128), F32),
            pltpu.VMEM((64, 128), F32),
            pltpu.VMEM((2, 32, 128), F32),
            pltpu.VMEM((2 * PER, 128), F32),
            pltpu.VMEM((CHUNKS, 2 * PER, 128), BF16),
            pltpu.VMEM((32, 348, 128), BF16),
            pltpu.VMEM((8, 128), jnp.int32),
            pltpu.VMEM((2, 32, 128), jnp.int32),
            pltpu.SMEM((2, 32, 128), jnp.int32),
            dma((2,)),
            dma,
            dma,
            dma,
            dma((NBLK,)),
            dma((NBLK,)),
            dma((NBLK,)),
            dma((NBLK,)),
            dma((CHUNKS, NBLK)),
            dma((CHUNKS, NBLK)),
        ],
        compiler_params=pltpu.CompilerParams(collective_id=0, has_side_effects=True),
        name="advance",
    )(
        micro_flags,
        load_plan,
        jnp.transpose(crm_state, (0, 2, 1, 3)),
        jnp.transpose(gcm_state, (0, 2, 1, 3)),
        h_mix,
        v_mix,
        to_crm,
        to_gcm.T,
        jnp.transpose(polar_tracer, (0, 2, 1)),
    )
    new_state, tendency, polar_next = pl.pallas_call(
        place,
        out_shape=(
            jax.ShapeDtypeStruct((2, 58, 32, 384), BF16),
            jax.ShapeDtypeStruct((2, 6, 32, 72), F32),
            jax.ShapeDtypeStruct((2, 32, 72), F32),
        ),
        in_specs=[smem] + [hbm] * 4 + [vmem] * 2,
        out_specs=(hbm, hbm, hbm),
        scratch_shapes=[
            pltpu.VMEM((32, 8, 128), jnp.int32),
            pltpu.VMEM((32, 2, 8, 128), F32),
            pltpu.VMEM((32, CHUNKS, 2 * PER, 128), BF16),
            pltpu.VMEM((2, 6, 32, 72), F32),
            pltpu.VMEM((2, 32, 72), F32),
            pltpu.VMEM((32, 348, 128), BF16),
            pltpu.VMEM((3, 2 * 58 * STEP, 128), F32),
            pltpu.VMEM((2, 58, 32, 384), BF16),
            pltpu.VMEM((2 * 6 * STEP, 128), F32),
            pltpu.VMEM((32, 8, 128), jnp.int32),
            pltpu.SMEM((32, 8, 128), jnp.int32),
            pltpu.VMEM((2, 1024, 128), F32),
            pltpu.VMEM((8, 128), jnp.int32),
            pltpu.VMEM((8, 128), F32),
            dma((3,)),
            dma((4,)),
            dma,
            dma((6,)),
        ],
        name="place",
    )(load_plan, recv, trec, prec, tbuf, courant_shift, courant_frac)
    return (
        jnp.transpose(new_state, (0, 2, 1, 3)),
        jnp.transpose(tendency, (0, 2, 1, 3)),
        jnp.transpose(polar_next, (0, 2, 1)),
    )


def solution(mesh):
    in_specs = (
        P("lat", "lon", None, None),
        P("lat", "lon", None, None),
        P("lat", "lon"),
        P("lat", "lon"),
        P(),
        P(),
        P(),
        P(),
        P("lat", None, "lon"),
        P("lat", None),
        P("lat", None),
    )
    out_specs = (P("lat", "lon", None, None), P("lat", "lon", None, None), P("lat", None, "lon"))
    return jax.shard_map(
        per_device, mesh=mesh, in_specs=in_specs, out_specs=out_specs, check_vma=False
    )
```

```python
import functools

import jax
import jax.numpy as jnp
from jax import lax
from jax.experimental import pallas as pl
from jax.experimental.pallas import tpu as pltpu
from jax.sharding import PartitionSpec as P

NSUB = 18
MESH = pl.DeviceIdType.MESH
F32 = jnp.float32
BF16 = jnp.bfloat16
HIGHEST = lax.Precision.HIGHEST

SIZES = (4, 4, 2)


def _hops(off):
    return sum(min(d, n - d) for d, n in zip(off, SIZES))


OFFSETS = sorted(
    ((a, b, c) for a in range(4) for b in range(4) for c in range(2)),
    key=lambda off: (-_hops(off), off),
)
NEAR = [(1, 1, 0), (3, 3, 0), (1, 0, 0), (3, 0, 0), (0, 1, 0), (0, 3, 0), (0, 0, 1), (0, 0, 0)]
OFFSETS = [off for off in OFFSETS if off not in NEAR] + NEAR
NBLK = len(OFFSETS)
CHUNKS = 4
PER = NBLK // CHUNKS
GROUPS = ((0, 8, 1, 9), (2, 3, 10, 11), (4, 5, 12, 13))
UNROLL = 18
MERGE = 3
STEP = 33


def _shifted(me, off):
    x, z, y = me // 8, (me // 2) % 4, me % 2
    return ((x + off[0]) % 4) * 8 + ((z + off[1]) % 4) * 2 + (y + off[2]) % 2


def _pick(index, values):
    out = jnp.int32(values[0])
    for i, value in enumerate(values[1:], 1):
        out = jnp.where(index == i, jnp.int32(value), out)
    return out


def _iota(shape, axis):
    return lax.broadcasted_iota(jnp.int32, shape, axis)


def _dot(a, b, **kw):
    return jnp.dot(a, b, preferred_element_type=F32, **kw)


def _onehot(mask):
    return jnp.where(mask, jnp.float32(1), jnp.float32(0)).astype(BF16)


def _part(r, t):
    return slice(58 * (3 * r + t), 58 * (3 * r + t) + 58)


def _lane_map(quarter, lanes):
    out = jnp.full(quarter.shape, lanes[0], jnp.int32)
    for i, lane in enumerate(lanes[1:], 1):
        out = jnp.where(quarter == i, lane, out)
    return out


def advance(
    flags,
    plan_in,
    crm,
    gcm_in,
    h_in,
    v_in,
    to_crm_in,
    to_gcm_in,
    tracer_in,
    recv,
    trec,
    prec,
    tend_out,
    plan_v,
    gcm,
    h_ref,
    v_ref,
    to_crm,
    to_gcm,
    tracer,
    tbuf,
    crm_v,
    cn,
    xs,
    x0,
    s0,
    fs,
    lf,
    gn,
    gsc,
    hbd,
    vbd,
    spread,
    gather,
    tc,
    tg,
    trt,
    updf,
    usend,
    snd,
    pack,
    order_v,
    order,
    small_sem,
    in_sem,
    order_sem,
    self_sem,
    tend_sem,
    ssem,
    rsem,
    pssem,
    prsem,
    tssem,
    trsem,
):
    me = lax.axis_index("lon")
    pairs = (
        (plan_in, plan_v),
        (h_in, h_ref),
        (v_in, v_ref),
        (to_crm_in, to_crm),
        (to_gcm_in, to_gcm),
        (tracer_in, tracer),
        (gcm_in, gcm),
    )
    smalls = [pltpu.make_async_copy(a, b, small_sem.at[n]) for n, (a, b) in enumerate(pairs)]
    for small in smalls:
        small.start()
    loads = [pltpu.make_async_copy(crm.at[r], crm_v.at[r], in_sem.at[r]) for r in range(2)]
    for load in loads:
        load.start()

    peers = [_shifted(me, off) for off in OFFSETS]
    barrier = pltpu.get_barrier_semaphore()
    for k in range(NBLK - 1):
        pl.semaphore_signal(barrier, inc=1, device_id={"lon": peers[k]}, device_id_type=MESH)

    smalls[0].wait()
    for r in range(2):
        owners = jnp.broadcast_to(plan_v[r : r + 1, :] // 32, (32, 32))
        at = jnp.where(owners == _iota((32, 32), 0), _iota((32, 32), 1), 0)
        order_v[r] = jnp.broadcast_to(jnp.max(at, axis=1, keepdims=True), (32, 128))
    lane = _iota((1, 128), 1)
    bound = jnp.full((1, 128), 64, jnp.int32)
    for k in range(NBLK):
        bound = jnp.where(lane // 2 == k, peers[k], bound)
    value = jnp.where(_iota((32, 128), 1) % 2 == 0, order_v[0], order_v[1] + 32)
    spot = jnp.where(bound == _iota((32, 128), 0), value, 0)
    pack[...] = jnp.zeros_like(pack)
    pack[0:2, 0:32] = plan_v[...]
    pack[2:3, :] = jnp.max(spot, axis=0, keepdims=True)
    to_smem = pltpu.make_async_copy(order_v, order, order_sem)
    to_smem.start()

    tile_h = _onehot(_iota((64, 256), 1) % 64 == _iota((64, 256), 0))
    tile_ht = _onehot(_iota((256, 64), 0) % 64 == _iota((256, 64), 1))
    tile_v = _onehot(_iota((58, 256), 1) % 64 == _iota((58, 256), 0))
    tile_vt = _onehot(_iota((256, 58), 0) % 64 == _iota((256, 58), 1))
    diag = _iota((256, 256), 0) // 64 == _iota((256, 256), 1) // 64
    smalls[1].wait()
    smalls[2].wait()
    h_rep = _dot(_dot(tile_ht, h_ref[...]).astype(BF16), tile_h)
    v_rep = _dot(_dot(tile_vt, v_ref[...]).astype(BF16), tile_v)
    hbd[...] = jnp.where(diag, h_rep, 0.0).astype(BF16)
    vbd[...] = jnp.where(diag, v_rep, 0.0).astype(BF16)
    for t, lanes in enumerate(GROUPS):
        spread[t] = _onehot(_iota((256, 256), 0) % 128 == _lane_map(_iota((256, 256), 1) // 64, lanes))
        hit = _iota((256, 128), 1) == _lane_map(_iota((256, 128), 0) // 64, lanes)
        gather[t * 256 : t * 256 + 256, :] = jnp.where(hit, jnp.float32(1.0 / 64), 0.0).astype(BF16)
    for small in smalls[3:]:
        small.wait()
    tc[...] = jnp.zeros_like(tc)
    tc[0:58, 0:72] = 0.5 * to_crm[...]
    tg[...] = jnp.zeros_like(tg)
    tg[0:58, 0:72] = to_gcm[...]
    gsc[...] = jnp.zeros_like(gsc)
    gn[...] = jnp.zeros_like(gn)
    xs[:, 48:64, :] = jnp.zeros((3 * PER, 16, 256), BF16)
    x0[:, 48:64, :] = jnp.zeros((3 * PER, 16, 256), BF16)
    s0[:, 56:64, :] = jnp.zeros((PER, 8, 256), F32)
    trt[...] = jnp.zeros_like(trt)
    for r in range(2):
        trt[r, :, 0:72] = tracer[r]
        for f in range(6):
            gn[(r * 6 + f) * STEP : (r * 6 + f) * STEP + 32, 0:72] = gcm[r, f].astype(F32)

    for r in range(2):
        loads[r].wait()

        def widen(level, carry):
            block = crm_v[r, level].astype(F32)
            for t in range(3):
                cn[t, pl.ds((r * 58 + level) * STEP, 32), :] = block[:, 128 * t : 128 * t + 128]
            return carry

        lax.fori_loop(0, 58, widen, 0, unroll=2)
    to_smem.wait()

    def pack_copy(k):
        return pltpu.make_async_remote_copy(
            src_ref=pack,
            dst_ref=prec.at[me],
            send_sem=pssem.at[k],
            recv_sem=prsem.at[k],
            device_id={"lon": peers[k]},
            device_id_type=MESH,
        )

    own_pack = pltpu.make_async_copy(pack, prec.at[me], pssem.at[NBLK - 1])
    own_pack.start()

    def tracer_copy(ch, k):
        return pltpu.make_async_remote_copy(
            src_ref=usend.at[ch],
            dst_ref=trec.at[me, ch],
            send_sem=tssem.at[ch, k],
            recv_sem=trsem.at[ch, k],
            device_id={"lon": peers[k]},
            device_id_type=MESH,
        )

    def own_tracer(ch):
        return pltpu.make_async_copy(usend.at[ch], trec.at[me, ch], tssem.at[ch, NBLK - 1])

    low58 = _iota((58, 128), 1) < 64
    low64 = _iota((64, 128), 1) < 64
    low1 = _iota((1, 128), 1) < 64

    def state_copy(k, dest):
        return pltpu.make_async_remote_copy(
            src_ref=snd.at[k],
            dst_ref=recv.at[me],
            send_sem=ssem.at[k],
            recv_sem=rsem.at[k],
            device_id={"lon": dest},
            device_id_type=MESH,
        )

    def chunk(ch, carry):
        dests = []
        for j in range(PER):
            offs = [OFFSETS[c * PER + j] for c in range(CHUNKS)]
            off = [_pick(ch, [o[i] for o in offs]) for i in range(3)]
            dests.append(_shifted(me, off))
        avs, bvs = [], []
        for p in range(PER):
            cols, a, b = [], [], []
            for r in range(2):
                i = order[r, dests[p], 0]
                cols.append([cn[t, pl.ds(r * 58 * STEP + i, 58, stride=STEP), :] for t in range(3)])
                row = 16 * p + 8 * r
                gsc[row : row + 6, :] = gn[pl.ds(r * 6 * STEP + i, 6, stride=STEP), :]
                flag = flags[r, i]
                a.append(jnp.where(flag == 1, jnp.float32(0.5), jnp.float32(0)))
                b.append(jnp.where(flag == 1, jnp.float32(0), jnp.float32(-0.25)))
            avs.append(jnp.where(low1, a[0], a[1]))
            bvs.append(jnp.where(low1, b[0], b[1]))
            one, two = cols[0][0], cols[1][0]
            first = jnp.where(low58, one, pltpu.roll(two, 64, 1))
            second = jnp.where(low58, pltpu.roll(one, 64, 1), two)
            s0[p, 0:58, 0:128] = first
            s0[p, 0:58, 128:256] = second
            blocks = ((first, second), (cols[0][1], cols[1][1]), (cols[0][2], cols[1][2]))
            for t in range(3):
                for half in range(2):
                    narrow = blocks[t][half].astype(BF16)
                    xs[t * PER + p, 0:58, 128 * half : 128 * half + 128] = narrow
                    x0[t * PER + p, 0:58, 128 * half : 128 * half + 128] = narrow
        forcing = lax.dot_general(
            tc[...],
            gsc[...],
            (((1,), (1,)), ((), ())),
            precision=HIGHEST,
            preferred_element_type=F32,
        )
        for p in range(PER):
            turned = forcing if p == 0 else pltpu.roll(forcing, 128 - 16 * p, 1)
            hi = turned.astype(BF16)
            lf[p, :, 0:128] = hi
            lf[p, :, 128:256] = (turned - hi.astype(F32)).astype(BF16)
        both = lf[...].reshape(PER * 64, 256)
        for t in range(3):
            fs[t * PER : t * PER + PER] = _dot(both, spread[t]).reshape(PER, 64, 256)

        def substep(step, carry):
            h, v = hbd[...], vbd[...]
            for m in range(0, 3 * PER // 4, MERGE):
                x = xs[4 * m : 4 * (m + MERGE)].reshape(MERGE * 256, 256)
                all_mixed = _dot(x, h).astype(BF16)
                for q in range(m, m + MERGE):
                    mixed = all_mixed[256 * (q - m) : 256 * (q - m) + 256]
                    grown = jnp.tanh(_dot(v, mixed))
                    for i in range(4):
                        c = 4 * q + i
                        new = grown[64 * i : 64 * i + 64] + fs[c]
                        if c < PER:
                            one, two = s0[c, :, 0:128], s0[c, :, 128:256]
                            adjust = jnp.tanh(one * two) * avs[c] + one * bvs[c]
                            first, second = new[:, 0:128] + adjust, new[:, 128:256] - adjust
                            s0[c, :, 0:128] = first
                            s0[c, :, 128:256] = second
                            xs[c, :, 0:128] = first.astype(BF16)
                            xs[c, :, 128:256] = second.astype(BF16)
                        else:
                            xs[c] = new.astype(BF16)
            return carry

        lax.fori_loop(0, NSUB, substep, 0, unroll=UNROLL)

        mean = jnp.zeros((PER * 64, 128), F32)
        for t in range(3):
            diff = (xs[t * PER : t * PER + PER] - x0[t * PER : t * PER + PER]).reshape(PER * 64, 256)
            mean += _dot(diff, gather[t * 256 : t * 256 + 256, :])
        total = mean[0:64]
        for p in range(1, PER):
            total += pltpu.roll(mean[64 * p : 64 * p + 64], 16 * p, 1)
        tend = _dot(jnp.transpose(total), tg[...], precision=HIGHEST)
        for p in range(PER):
            for r in range(2):
                row = 16 * p + 8 * r
                tbuf[dests[p], r] = tend[row : row + 8]
                home = pl.ds(order[r, dests[p], 0], 1)
                updf[2 * p + r : 2 * p + r + 1, :] = tend[row : row + 1] + trt[r, home, :]
        usend[ch] = updf[...].astype(BF16)

        for p in range(PER):
            k = ch * PER + p
            one, two = s0[p, :, 0:128], s0[p, :, 128:256]
            left = jnp.where(low64, one, pltpu.roll(two, 64, 1)).astype(BF16)
            right = jnp.where(low64, pltpu.roll(one, 64, 1), two).astype(BF16)
            snd[k, _part(0, 0), :] = left[0:58]
            snd[k, _part(1, 0), :] = right[0:58]
            for t in (1, 2):
                for r in range(2):
                    snd[k, _part(r, t), :] = xs[t * PER + p, 0:58, 128 * r : 128 * r + 128]

        @pl.when(ch == 0)
        def _():
            pl.semaphore_wait(barrier, NBLK - 1)
            for k in range(NBLK - 1):
                pack_copy(k).start()

        for k in range(NBLK - 1):
            tracer_copy(ch, k).start()
        own_tracer(ch).start()
        for j in range(PER - 1):
            state_copy(ch * PER + j, dests[j]).start()

        @pl.when(ch < CHUNKS - 1)
        def _():
            state_copy(ch * PER + PER - 1, dests[PER - 1]).start()

        return carry

    lax.fori_loop(0, CHUNKS, chunk, 0)

    own_state = pltpu.make_async_copy(snd.at[NBLK - 1], recv.at[me], self_sem)
    own_state.start()
    tend_copy = pltpu.make_async_copy(tbuf, tend_out, tend_sem)
    tend_copy.start()

    tend_copy.wait()
    own_state.wait()
    own_pack.wait()
    for ch in range(CHUNKS):
        own_tracer(ch).wait()
    for k in range(NBLK - 1):
        pack_copy(k).wait()
        state_copy(k, peers[k]).wait()
        for ch in range(CHUNKS):
            tracer_copy(ch, k).wait()


def place(
    plan_s,
    recv,
    trec_hbm,
    prec_hbm,
    tbuf_hbm,
    shift,
    frac,
    state_out,
    tend_out,
    polar_out,
    prec,
    tbuf,
    trec,
    tend_v,
    polar_v,
    rbuf,
    wide,
    obuf,
    tn,
    slots_v,
    slots_s,
    loop,
    cs,
    cf,
    small_sem,
    in_sem,
    slot_sem,
    out_sem,
):
    me = lax.axis_index("lon")
    smalls = [
        pltpu.make_async_copy(src, dst, small_sem.at[n])
        for n, (src, dst) in enumerate(((prec_hbm, prec), (tbuf_hbm, tbuf), (trec_hbm, trec)))
    ]
    loads = [
        pltpu.make_async_copy(recv.at[pl.ds(8 * q, 8)], rbuf.at[pl.ds(8 * q, 8)], in_sem.at[q])
        for q in range(4)
    ]
    for load in smalls + loads:
        load.start()
    smalls[0].wait()
    plans = prec[...]
    held = (plans // 32 == me) & (_iota((32, 8, 128), 2) < 32) & (_iota((32, 8, 128), 1) < 2)
    mine = jnp.where(held, plans % 32, 0)
    slots_v[...] = jnp.broadcast_to(jnp.max(mine, axis=2, keepdims=True), (32, 8, 128))
    to_smem = pltpu.make_async_copy(slots_v, slots_s, slot_sem)
    to_smem.start()
    smalls[1].wait()

    for r in range(2):
        for i in range(32):
            tn[pl.ds(r * 6 * STEP + i, 6, stride=STEP), :] = tbuf[plan_s[r, i] // 32, r, 0:6, :]
        for f in range(6):
            at = (r * 6 + f) * STEP
            tend_v[r, f] = tn[at : at + 32, 0:72]
    outs = [pltpu.make_async_copy(tend_v, tend_out, out_sem.at[4])]
    outs[0].start()

    smalls[2].wait()
    target = _iota((64, 64), 0)
    for s in range(32):
        spots = jnp.broadcast_to(prec[s, 2:3, 0:64], (64, 64))
        rows = _dot(_onehot(spots == target), trec[s].reshape(64, 128))
        for r in range(2):
            loop[r, 32 * s : 32 * s + 32, :] = rows[32 * r : 32 * r + 32]

    to_smem.wait()
    for load in loads:
        load.wait()
    for r in range(2):

        def spot(s, carry):
            at = pl.ds(r * 58 * STEP + slots_s[s, r, 0], 58, stride=STEP)
            for t in range(3):
                wide[t, at, :] = rbuf[s, _part(r, t), :].astype(F32)
            return carry

        lax.fori_loop(0, 32, spot, 0, unroll=4)
        for part in range(2):
            for level in range(29 * part, 29 * part + 29):
                for t in range(3):
                    at = (r * 58 + level) * STEP
                    obuf[r, level, :, 128 * t : 128 * t + 128] = wide[t, at : at + 32, :].astype(BF16)
            piece = pl.ds(29 * part, 29)
            outs.append(
                pltpu.make_async_copy(
                    obuf.at[r, piece], state_out.at[r, piece], out_sem.at[2 * r + part]
                )
            )
            outs[-1].start()

    cs[...] = jnp.zeros_like(cs)
    cf[...] = jnp.zeros_like(cf)
    cs[0:2, 0:72] = shift[...]
    cf[0:2, 0:72] = frac[...]
    for r in range(2):
        base = (me * 32 - 1 - cs[r : r + 1, :]) & 1023
        whole = loop[r]
        cut = jnp.concatenate([whole[512:1024], whole[0:32]], axis=0)
        now = jnp.where((base & 512) != 0, cut, whole[0:544])
        for size in (256, 128, 64, 32, 16, 8):
            rows = size + 32
            now = jnp.where((base & size) != 0, now[size : size + rows], now[0:rows])
        for size in (4, 2, 1):
            now = jnp.where((base & size) != 0, pltpu.roll(now, 40 - size, 0), now)
        weight = cf[r : r + 1, :]
        result = (1.0 - weight) * pltpu.roll(now, 39, 0) + weight * now
        polar_v[r] = result[0:32, 0:72]
    outs.append(pltpu.make_async_copy(polar_v, polar_out, out_sem.at[5]))
    outs[-1].start()

    for out in outs:
        out.wait()


def per_device(
    crm_state,
    gcm_state,
    micro_flags,
    load_plan,
    h_mix,
    v_mix,
    to_crm,
    to_gcm,
    polar_tracer,
    courant_shift,
    courant_frac,
):
    smem = pl.BlockSpec(memory_space=pltpu.SMEM)
    vmem = pl.BlockSpec(memory_space=pltpu.VMEM)
    hbm = pl.BlockSpec(memory_space=pl.ANY)
    dma = pltpu.SemaphoreType.DMA
    recv, trec, prec, tbuf = pl.pallas_call(
        advance,
        out_shape=(
            jax.ShapeDtypeStruct((32, 348, 128), BF16),
            jax.ShapeDtypeStruct((32, CHUNKS, 2 * PER, 128), BF16),
            jax.ShapeDtypeStruct((32, 8, 128), jnp.int32),
            jax.ShapeDtypeStruct((32, 2, 8, 128), F32),
        ),
        in_specs=[smem] + [hbm] * 8,
        out_specs=(hbm, hbm, hbm, hbm),
        scratch_shapes=[
            pltpu.VMEM((2, 32), jnp.int32),
            pltpu.VMEM((2, 6, 32, 72), BF16),
            pltpu.VMEM((64, 64), BF16),
            pltpu.VMEM((58, 58), BF16),
            pltpu.VMEM((58, 72), F32),
            pltpu.VMEM((58, 72), F32),
            pltpu.VMEM((2, 32, 72), F32),
            pltpu.VMEM((32, 2, 8, 128), F32),
            pltpu.VMEM((2, 58, 32, 384), BF16),
            pltpu.VMEM((3, 2 * 58 * STEP, 128), F32),
            pltpu.VMEM((3 * PER, 64, 256), BF16),
            pltpu.VMEM((3 * PER, 64, 256), BF16),
            pltpu.VMEM((PER, 64, 256), F32),
            pltpu.VMEM((3 * PER, 64, 256), F32),
            pltpu.VMEM((PER, 64, 256), BF16),
            pltpu.VMEM((2 * 6 * STEP, 128), F32),
            pltpu.VMEM((128, 128), F32),
            pltpu.VMEM((256, 256), BF16),
            pltpu.VMEM((256, 256), BF16),
            pltpu.VMEM((3, 256, 256), BF16),
            pltpu.VMEM((768, 128), BF16),
            pltpu.VMEM((64, 128), F32),
            pltpu.VMEM((64, 128), F32),
            pltpu.VMEM((2, 32, 128), F32),
            pltpu.VMEM((2 * PER, 128), F32),
            pltpu.VMEM((CHUNKS, 2 * PER, 128), BF16),
            pltpu.VMEM((32, 348, 128), BF16),
            pltpu.VMEM((8, 128), jnp.int32),
            pltpu.VMEM((2, 32, 128), jnp.int32),
            pltpu.SMEM((2, 32, 128), jnp.int32),
            dma((7,)),
            dma((2,)),
            dma,
            dma,
            dma,
            dma((NBLK,)),
            dma((NBLK,)),
            dma((NBLK,)),
            dma((NBLK,)),
            dma((CHUNKS, NBLK)),
            dma((CHUNKS, NBLK)),
        ],
        compiler_params=pltpu.CompilerParams(collective_id=0, has_side_effects=True),
        name="advance",
    )(
        micro_flags,
        load_plan,
        jnp.transpose(crm_state, (0, 2, 1, 3)),
        jnp.transpose(gcm_state, (0, 2, 1, 3)),
        h_mix,
        v_mix,
        to_crm,
        to_gcm.T,
        jnp.transpose(polar_tracer, (0, 2, 1)),
    )
    new_state, tendency, polar_next = pl.pallas_call(
        place,
        out_shape=(
            jax.ShapeDtypeStruct((2, 58, 32, 384), BF16),
            jax.ShapeDtypeStruct((2, 6, 32, 72), F32),
            jax.ShapeDtypeStruct((2, 32, 72), F32),
        ),
        in_specs=[smem] + [hbm] * 4 + [vmem] * 2,
        out_specs=(hbm, hbm, hbm),
        scratch_shapes=[
            pltpu.VMEM((32, 8, 128), jnp.int32),
            pltpu.VMEM((32, 2, 8, 128), F32),
            pltpu.VMEM((32, CHUNKS, 2 * PER, 128), BF16),
            pltpu.VMEM((2, 6, 32, 72), F32),
            pltpu.VMEM((2, 32, 72), F32),
            pltpu.VMEM((32, 348, 128), BF16),
            pltpu.VMEM((3, 2 * 58 * STEP, 128), F32),
            pltpu.VMEM((2, 58, 32, 384), BF16),
            pltpu.VMEM((2 * 6 * STEP, 128), F32),
            pltpu.VMEM((32, 8, 128), jnp.int32),
            pltpu.SMEM((32, 8, 128), jnp.int32),
            pltpu.VMEM((2, 1024, 128), F32),
            pltpu.VMEM((8, 128), jnp.int32),
            pltpu.VMEM((8, 128), F32),
            dma((3,)),
            dma((4,)),
            dma,
            dma((6,)),
        ],
        name="place",
    )(load_plan, recv, trec, prec, tbuf, courant_shift, courant_frac)
    return (
        jnp.transpose(new_state, (0, 2, 1, 3)),
        jnp.transpose(tendency, (0, 2, 1, 3)),
        jnp.transpose(polar_next, (0, 2, 1)),
    )


def solution(mesh):
    in_specs = (
        P("lat", "lon", None, None),
        P("lat", "lon", None, None),
        P("lat", "lon"),
        P("lat", "lon"),
        P(),
        P(),
        P(),
        P(),
        P("lat", None, "lon"),
        P("lat", None),
        P("lat", None),
    )
    out_specs = (P("lat", "lon", None, None), P("lat", "lon", None, None), P("lat", None, "lon"))
    return jax.shard_map(
        per_device, mesh=mesh, in_specs=in_specs, out_specs=out_specs, check_vma=False
    )
```
